256 devices in a mesh: layer: 4 (over z_hi), feat: 64 (over z_lo, y, x, core).
Axes of the slice: x: 4, y: 4, z: 8 (z_hi: 4, z_lo: 2; z = z_hi * 2 + z_lo), core: 2. Of those that a mesh axis runs over, the one named last changes fastest.
Arguments:
- residuals: bfloat16 [4, 512, 4608], P('layer', 'feat'), may hold values from -60 to 60
- enc_weight: bfloat16 [4, 4608, 16384], P('layer', None, 'feat'), may hold values from -0.09375 to 0.09375
- enc_bias: float32 [4, 16384], P('layer', 'feat'), may hold values from -3 to 3
- thresh_levels: int32 [4, 16384], P('layer', 'feat'), may hold values from 2 to 8
- dec_weight: bfloat16 [4, 4, 4608, 16384], P('layer', None, 'feat'), may hold values from -0.046875 to 0.046875
- dec_bias: float32 [4, 4608], P('layer', 'feat'), may hold values from -3 to 3
Outputs:
- recon: bfloat16 [4, 512, 4608], P('layer', None, 'feat')
The draws below stay inside these ranges and needn't reach their ends.
All inputs are finite; a program needn't handle non-finite values.
Results may differ from the reference program's by a relative error of at most 0.0053.
Values may be sent and summed in bfloat16 or wider, within the bound.
No kernel may reach another device: no remote copies, remote signals or barrier semaphores. Data moves between devices by JAX's collectives and lax.ppermute only.
A program may use at most 128 MiB of HBM per device.

```python
import math
import jax
import jax.numpy as jnp
from jax import lax

D = 4608
FEATURES = 16384
LAYERS = 4
TOKENS = 512


def draw_residuals(key, part):
    first_key, second_key = jax.random.split(jax.random.fold_in(key, 11))
    base = jnp.clip(jax.random.normal(first_key, (LAYERS, TOKENS, D), jnp.float32), -6.0, 6.0)
    scales = jnp.exp(jax.random.uniform(second_key, (LAYERS, TOKENS, 1), jnp.float32, 0.0, math.log(10.0)))
    return (base * scales).astype(jnp.bfloat16)


def dense_groups(key):
    block_size = 64
    groups = FEATURES // block_size
    chosen = max(1, groups // 4)
    layer_keys = jax.random.split(jax.random.fold_in(key, 23), LAYERS)

    def order_one(layer_key):
        return jax.random.permutation(layer_key, groups)
    orders = jax.vmap(order_one)(layer_keys)
    marks = orders < chosen
    return jnp.repeat(marks, block_size, axis=1)


def draw_thresh_levels(key, part):
    dense = dense_groups(key)
    levels = jax.random.randint(jax.random.fold_in(key, 31), (LAYERS, FEATURES), 2, 9)
    return jnp.where(dense, 2, levels).astype(jnp.int32)


def draw_enc_bias(key, part):
    dense = dense_groups(key)
    first_key, second_key = jax.random.split(jax.random.fold_in(key, 37))
    spread = jnp.clip(0.5 * jax.random.normal(first_key, (LAYERS, FEATURES), jnp.float32), -3.0, 3.0)
    high = jax.random.uniform(second_key, (LAYERS, FEATURES), jnp.float32, 2.0, 3.0)
    return jnp.where(dense, high, spread).astype(jnp.float32)


def steps_of(own_key, shape, cuts, least, top_value):
    def one(axis_at, parts):
        steps = jax.random.uniform(jax.random.fold_in(jax.random.fold_in(own_key, 6), axis_at), (parts,), jnp.float32, least / len(cuts), top_value / len(cuts))
        return jnp.repeat(jnp.exp(steps), shape[axis_at] // parts).reshape((-1,) + (1,) * (len(shape) - axis_at - 1))

    level = one(*cuts[0])
    for cut in cuts[1:]:
        level = level * one(*cut)
    return level


def centred(own_key, shape, deviation, limit, pieces=(), dtype=jnp.bfloat16):
    values = jax.random.normal(own_key, shape, jnp.float32) * deviation
    if len(pieces) > 0:
        values = steps_of(own_key, shape, pieces, -0.22, 0.18) * values
    return jnp.clip(values, min=-limit, max=limit).astype(dtype)


def setup_inputs(seed: int = 0) -> dict:
    keys = jax.random.split(jax.random.key(seed), 7)
    return {
        "residuals": draw_residuals(jax.random.fold_in(keys[6], 71), 0),
        "enc_weight": centred(keys[1], (LAYERS, D, FEATURES), D ** -0.5, 0.09375, ((0, 4), (2, 64))),
        "enc_bias": draw_enc_bias(jax.random.fold_in(keys[6], 71), 0),
        "thresh_levels": draw_thresh_levels(jax.random.fold_in(keys[6], 71), 0),
        "dec_weight": centred(keys[4], (LAYERS, LAYERS, D, FEATURES), FEATURES ** -0.5, 0.046875, ((0, 4), (2, 64))),
        "dec_bias": centred(keys[5], (LAYERS, D), 0.5, 3.0, ((0, 4), (1, 64)), jnp.float32),
    }


def encode(resid, enc_matrix, bias_row, levels):
    resid_float = resid.astype(jnp.float32)
    factor = lax.rsqrt(lax.optimization_barrier(jnp.mean(resid_float * resid_float, axis=-1, keepdims=True)) + 1e-06)
    normed = (resid_float * factor).astype(jnp.bfloat16)
    pre = jnp.dot(normed, enc_matrix, preferred_element_type=jnp.float32) + bias_row
    theta = levels.astype(jnp.float32) * 0.125
    return (pre * jnp.clip((pre - theta) / 0.25, 0.0, 1.0)).astype(jnp.bfloat16)

def reference(residuals, enc_weight, enc_bias, thresh_levels, dec_weight, dec_bias):
    activations = [encode(residuals[i], enc_weight[i], enc_bias[i], thresh_levels[i]) for i in range(LAYERS)]
    results = []
    for target in range(LAYERS):
        total = jnp.zeros((TOKENS, D), jnp.float32)
        for source in range(target + 1):
            total = total + jnp.dot(activations[source], dec_weight[source, target].T, preferred_element_type=jnp.float32)
        results.append((total + dec_bias[target]).astype(jnp.bfloat16))
    return jnp.stack(results)
```

```python
import jax
import jax.numpy as jnp
import numpy as np
from jax import lax
from jax.experimental import pallas as pl
from jax.experimental.pallas import tpu as pltpu
from jax.sharding import PartitionSpec as P

NZ, NY, NX = 2, 4, 4


def place(z, y, x, c):
    return (z % NZ) * 32 + (y % NY) * 8 + (x % NX) * 2 + c


ALL = [(z, y, x, c) for z in range(NZ) for y in range(NY) for x in range(NX) for c in range(2)]


def along(c, first, second, z):
    return place(z, second, first, c) if c == 0 else place(z, first, second, c)


GROUPS_A = [[along(c, p, q, z) for p in range(4) for z in range(2)] for c in range(2) for q in range(4)]
GROUPS_1 = [[along(c, p, q, z) for p in range(4)] for c in range(2) for z in range(2) for q in range(4)]
GROUPS_2 = [[along(c, p, q, z) for q in range(4)] for c in range(2) for z in range(2) for p in range(4)]
SWAP_CORE = [(place(z, y, x, c), place(z, y, x, 1 - c)) for z, y, x, c in ALL]
SWAP_Z = [(place(z, y, x, c), place(1 - z, y, x, c)) for z, y, x, c in ALL]


def shift2(s):
    return [
        (along(c, p, q, z), along(c, p, (q + s) % 4, z))
        for c in range(2)
        for z in range(2)
        for p in range(4)
        for q in range(4)
    ]


def table():
    rows = np.zeros((64, 40), np.int32)
    for z, y, x, c in ALL:
        p, q = (x, y) if c == 0 else (y, x)
        row = [c]
        for s in range(4):
            for p1 in range(4):
                for j in range(2):
                    q2 = (q - s) % 4
                    yy, xx = (q2, p1) if c == 0 else (p1, q2)
                    row.append((z ^ j) * 16 + yy * 4 + xx)
        rows[place(z, y, x, c), : len(row)] = row
    return rows


TABLE = table()
KSTEPS = 6


def encode_body(info, x, w_own, w_other, vec_own, vec_other, out, acc):
    k = pl.program_id(0)

    @pl.when(k == 0)
    def _():
        acc[...] = jnp.zeros_like(acc)

    acc[0] += jnp.dot(x[...], w_own[...], preferred_element_type=jnp.float32)
    acc[1] += jnp.dot(x[...], w_other[...], preferred_element_type=jnp.float32)

    def gate(pre, vec):
        pre = pre + vec[0:1, :]
        return (pre * jnp.clip((pre - vec[1:2, :]) / 0.25, 0.0, 1.0)).astype(jnp.bfloat16)

    def store(c):
        for i, vec in ((0, vec_own), (1, vec_other)):
            col = (c ^ i) * 256
            act = gate(acc[i], vec)
            if c == 0:
                out[:, col : col + 256] = act
            else:
                for b in range(16):
                    d = (b % 4) * 4 + b // 4
                    out[d * 16 : d * 16 + 16, col : col + 256] = act[b * 16 : b * 16 + 16]

    for c in range(2):

        @pl.when((k == KSTEPS - 1) & (info[0] == c))
        def _(c=c):
            store(c)


def encode(info, x, w_own, w_other, vec_own, vec_other):
    kb = x.shape[1] // KSTEPS
    return pl.pallas_call(
        encode_body,
        out_shape=jax.ShapeDtypeStruct((256, 512), jnp.bfloat16),
        grid_spec=pltpu.PrefetchScalarGridSpec(
            num_scalar_prefetch=1,
            grid=(KSTEPS,),
            in_specs=[
                pl.BlockSpec((256, kb), lambda k, t: (0, k)),
                pl.BlockSpec((kb, 256), lambda k, t: (k, 0)),
                pl.BlockSpec((kb, 256), lambda k, t: (k, 0)),
                pl.BlockSpec((8, 256), lambda k, t: (0, 0)),
                pl.BlockSpec((8, 256), lambda k, t: (0, 0)),
            ],
            out_specs=pl.BlockSpec((256, 512), lambda k, t: (0, 0)),
            scratch_shapes=[pltpu.VMEM((2, 256, 256), jnp.float32)],
        ),
        name="encode",
    )(info, x, w_own, w_other, vec_own, vec_other)


def decode(info, pieces, offsets, w_own, w_other, acc):
    counts = [p.shape[0] for p in pieces]
    starts = [sum(counts[:i]) for i in range(len(counts))]
    total = sum(counts)

    def chunk(k, t):
        at = 0
        for n, (s, off) in enumerate(zip(starts, offsets)):
            here = t[1 + off + jnp.clip(k - s, 0, counts[n] - 1)]
            at = here if n == 0 else jnp.where(k >= s, here, at)
        return at

    def body(info, *refs):
        acts, (wo, wp), rest = refs[: len(pieces)], refs[len(pieces) : len(pieces) + 2], refs[len(pieces) + 2 :]
        out = rest[-1]
        k = pl.program_id(0)

        @pl.when(k == 0)
        def _():
            out[...] = jnp.zeros_like(out) if acc is None else rest[0][...]

        def add(a):
            dims = (((1,), (1,)), ((), ()))
            out[0] += lax.dot_general(wo[...], a, dims, preferred_element_type=jnp.float32)
            out[1] += lax.dot_general(wp[...], a, dims, preferred_element_type=jnp.float32)

        for n, a in enumerate(acts):
            if len(pieces) == 1:
                add(a[0])
            else:

                @pl.when((k >= starts[n]) & (k < starts[n] + counts[n]))
                def _(a=a):
                    add(a[0])

    specs = [
        pl.BlockSpec((1, 256, 512), lambda k, t, s=s, n=n: (jnp.clip(k - s, 0, n - 1), 0, 0))
        for s, n in zip(starts, counts)
    ]
    specs += [pl.BlockSpec((288, 512), lambda k, t: (0, chunk(k, t)))] * 2
    whole = pl.BlockSpec((2, 288, 256), lambda k, t: (0, 0, 0))
    args = [info, *pieces, w_own, w_other]
    if acc is not None:
        specs.append(whole)
        args.append(acc)
    return pl.pallas_call(
        body,
        out_shape=jax.ShapeDtypeStruct((2, 288, 256), jnp.float32),
        grid_spec=pltpu.PrefetchScalarGridSpec(
            num_scalar_prefetch=1, grid=(total,), in_specs=specs, out_specs=whole
        ),
        name="decode",
    )(*args)


def per_device(residuals, enc_weight, enc_bias, thresh_levels, dec_weight, dec_bias):
    me, my_layer = lax.axis_index("feat"), lax.axis_index("layer")
    info = lax.dynamic_index_in_dim(jnp.asarray(TABLE), me, 0, keepdims=False)
    layers, width, features = dec_weight.shape[1:]

    vec = jnp.concatenate(
        [enc_bias, thresh_levels.astype(jnp.float32) * 0.125, jnp.pad(dec_bias, ((0, 0), (0, 256 - width)))], 0
    )
    vec = jnp.pad(vec, ((0, 5), (0, 0)))
    vec_other = lax.ppermute(vec, "feat", SWAP_CORE)
    enc_own = enc_weight[0]
    enc_other = lax.ppermute(enc_own, "feat", SWAP_CORE)
    dec_own = dec_weight[0].reshape(layers * width, features)
    dec_other = lax.ppermute(dec_own, "feat", SWAP_CORE)

    resid = residuals[0].astype(jnp.float32)
    factor = lax.rsqrt(jnp.mean(resid * resid, axis=-1, keepdims=True) + 1e-06)
    normed = (resid * factor).astype(jnp.bfloat16)
    rows = lax.all_to_all(
        jnp.broadcast_to(normed[None], (8, *normed.shape)), "feat", 0, 0, axis_index_groups=GROUPS_A
    )
    rows = lax.all_to_all(jnp.broadcast_to(rows[None], (4, *rows.shape)), "feat", 0, 0, axis_index_groups=GROUPS_2)
    rows = rows.reshape(256, normed.shape[1])

    acts = encode(info, rows, enc_own, enc_other, vec, vec_other)

    acts_z = lax.ppermute(acts, "feat", SWAP_Z)
    pair = jnp.stack([acts, acts_z])
    ring = lax.all_to_all(jnp.broadcast_to(pair[None], (4, *pair.shape)), "feat", 0, 0, axis_index_groups=GROUPS_1)
    half1, half2 = ring[:2].reshape(4, 256, 512), ring[2:].reshape(4, 256, 512)
    left1 = lax.ppermute(half1, "feat", shift2(1))
    right2 = lax.ppermute(half2, "feat", shift2(-1))
    left2 = lax.ppermute(half2, "feat", shift2(1))
    right1 = lax.ppermute(half1, "feat", shift2(-1))
    far1 = lax.ppermute(left1, "feat", shift2(1))
    far2 = lax.ppermute(right2, "feat", shift2(-1))

    part = decode(info, [half1, half2], [0, 4], dec_own, dec_other, None)
    part = decode(info, [left1, right2], [8, 28], dec_own, dec_other, part)
    part = decode(info, [left2, right1], [12, 24], dec_own, dec_other, part)
    part = decode(info, [far1, far2], [16, 20], dec_own, dec_other, part)

    part = part.reshape(2, layers, width, 256)
    total = lax.dynamic_index_in_dim(part, my_layer, 1, keepdims=False)
    for step in range(1, layers):
        sent = lax.dynamic_index_in_dim(part, jnp.minimum(my_layer + step, layers - 1), 1, keepdims=False)
        total = total + lax.ppermute(sent, "layer", [(s, s + step) for s in range(layers - step)])
    bias = jnp.stack([vec[2, :width], vec_other[2, :width]])[:, :, None]
    total = (total + bias).astype(jnp.bfloat16)

    theirs = lax.ppermute(total[1], "feat", SWAP_CORE)
    mine = total[0]
    first = info[0] == 0
    both = jnp.stack([jnp.where(first, mine, theirs), jnp.where(first, theirs, mine)])
    both = both.reshape(2, width, NY, NX, NZ, 8).transpose(4, 2, 3, 0, 5, 1)
    return both.reshape(1, 512, width)


def solution(mesh):
    in_specs = (
        P("layer", "feat", None),
        P("layer", None, "feat"),
        P("layer", "feat"),
        P("layer", "feat"),
        P("layer", None, "feat", None),
        P("layer", "feat"),
    )
    out_specs = P("layer", None, "feat")
    return jax.shard_map(
        per_device, mesh=mesh, in_specs=in_specs, out_specs=out_specs, check_vma=False
    )
```

```python
import jax
import jax.numpy as jnp
import numpy as np
from jax import lax
from jax.experimental import pallas as pl
from jax.experimental.pallas import tpu as pltpu
from jax.sharding import PartitionSpec as P


NZ, NY, NX = 2, 4, 4


def place(z, y, x, c):
    return (z % NZ) * 32 + (y % NY) * 8 + (x % NX) * 2 + c


ALL = [(z, y, x, c) for z in range(NZ) for y in range(NY) for x in range(NX) for c in range(2)]


def along(c, first, second, z):
    return place(z, second, first, c) if c == 0 else place(z, first, second, c)


SWAP_CORE = [(place(z, y, x, c), place(z, y, x, 1 - c)) for z, y, x, c in ALL]
SWAP_Z = [(place(z, y, x, c), place(1 - z, y, x, c)) for z, y, x, c in ALL]
RING = [(c, z, p, q) for c in range(2) for z in range(2) for p in range(4) for q in range(4)]


def shift1(s):
    return [(along(c, p, q, z), along(c, (p + s) % 4, q, z)) for c, z, p, q in RING]


def shift2(s):
    return [(along(c, p, q, z), along(c, p, (q + s) % 4, z)) for c, z, p, q in RING]


def table():
    rows = np.zeros((64, 40), np.int32)
    for z, y, x, c in ALL:
        p, q = (x, y) if c == 0 else (y, x)
        row = [c]
        for s2 in range(4):
            for s1 in range(4):
                for j in range(2):
                    p1, q2 = (p - s1) % 4, (q - s2) % 4
                    yy, xx = (q2, p1) if c == 0 else (p1, q2)
                    row.append((z ^ j) * 16 + yy * 4 + xx)
        rows[place(z, y, x, c), : len(row)] = row
    return rows


TABLE = table()
KSTEPS = 2


def encode_body(info, x0, x1, x2, x3, w_own, w_other, vec_own, vec_other, out, acc):
    k = pl.program_id(0)
    x = jnp.concatenate([x0[...], x1[...], x2[...], x3[...]], 0)
    for i, w in ((0, w_own), (1, w_other)):
        prod = jnp.dot(x, w[...], preferred_element_type=jnp.float32)

        @pl.when(k == 0)
        def _(i=i, prod=prod):
            acc[i] = prod

        @pl.when(k > 0)
        def _(i=i, prod=prod):
            acc[i] += prod

    @pl.when(k == KSTEPS - 1)
    def _():
        for i, vec in ((0, vec_own), (1, vec_other)):
            pre = acc[i] + vec[0:1, :]
            acc[i] = pre * jnp.clip((pre - vec[1:2, :]) / 0.25, 0.0, 1.0)
        for i in range(2):
            col = pl.multiple_of((info[0] ^ i) * 256, 256)
            for b in range(32):
                row = pl.multiple_of(info[1 + b] * 8, 8)
                acc[2 + i, pl.ds(row, 8), :] = acc[i, b * 8 : b * 8 + 8, :]
            out[:, pl.ds(col, 256)] = acc[2 + i].astype(jnp.bfloat16)


def encode(info, xs, w_own, w_other, vec_own, vec_other):
    kb = xs[0].shape[1] // KSTEPS
    return pl.pallas_call(
        encode_body,
        out_shape=jax.ShapeDtypeStruct((256, 512), jnp.bfloat16),
        grid_spec=pltpu.PrefetchScalarGridSpec(
            num_scalar_prefetch=1,
            grid=(KSTEPS,),
            in_specs=[pl.BlockSpec((64, kb), lambda k, t: (0, k))] * 4
            + [pl.BlockSpec((kb, 256), lambda k, t: (k, 0))] * 2
            + [pl.BlockSpec((8, 256), lambda k, t: (0, 0))] * 2,
            out_specs=pl.BlockSpec((256, 512), lambda k, t: (0, 0)),
            scratch_shapes=[pltpu.VMEM((4, 256, 256), jnp.float32)],
        ),
        compiler_params=pltpu.CompilerParams(vmem_limit_bytes=20 << 20),
        name="encode",
    )(info, *xs, w_own, w_other, vec_own, vec_other)


def decode(info, pieces, offsets, w_own, w_other, acc, last=False):
    n_in = len(pieces) + 2 + (acc is not None)

    def body(info, *refs):
        acts, (wo, wp) = refs[: len(pieces)], refs[len(pieces) : len(pieces) + 2]
        out = refs[n_in]
        for h, w in ((0, wo), (1, wp)):
            total = None if acc is None else refs[n_in - 1][h]
            for a, off in zip(acts, offsets):
                for i in range(a.shape[0]):
                    place_of = off[i // 2] + i % 2 if isinstance(off, tuple) else off + i
                    col = pl.multiple_of(info[1 + place_of] * 512, 512)
                    part = lax.dot_general(
                        w[:, pl.ds(col, 512)], a[i], (((1,), (1,)), ((), ())), preferred_element_type=jnp.float32
                    )
                    total = part if total is None else total + part
            out[h] = total
            if last:
                sent = refs[n_in + 1]
                for e in range(4):
                    sent[e, h] = out[h, e * 72 : e * 72 + 72, :].astype(jnp.bfloat16)

    vmem = pl.BlockSpec(memory_space=pltpu.VMEM)
    args = [*pieces, w_own, w_other] + ([] if acc is None else [acc])
    args = [pltpu.with_memory_space_constraint(v, pltpu.VMEM) for v in args]
    shapes = [jax.ShapeDtypeStruct((2, 288, 256), jnp.float32)]
    if last:
        shapes.append(jax.ShapeDtypeStruct((4, 2, 72, 256), jnp.bfloat16))
    return pl.pallas_call(
        body,
        out_shape=shapes,
        in_specs=[pl.BlockSpec(memory_space=pltpu.SMEM)] + [vmem] * len(args),
        out_specs=[vmem] * len(shapes),
        compiler_params=pltpu.CompilerParams(vmem_limit_bytes=16 << 20),
        name="decode",
    )(info, *args)


def fetch(x):
    return pl.pallas_call(
        lambda src, dst: pltpu.sync_copy(src, dst),
        out_shape=jax.ShapeDtypeStruct(x.shape, x.dtype),
        in_specs=[pl.BlockSpec(memory_space=pl.ANY)],
        out_specs=pl.BlockSpec(memory_space=pltpu.VMEM),
        compiler_params=pltpu.CompilerParams(vmem_limit_bytes=16 << 20),
        name="fetch",
    )(x)


def work(residuals, enc_weight, enc_bias, thresh_levels, dec_weight, dec_bias):
    me, my_layer = lax.axis_index("feat"), lax.axis_index("layer")
    info = lax.dynamic_index_in_dim(jnp.asarray(TABLE), me, 0, keepdims=False)
    layers, width, features = dec_weight.shape[1:]

    def send(x, pairs):
        return lax.ppermute(x, "feat", pairs)

    resid = residuals[0].astype(jnp.float32)
    factor = lax.rsqrt(jnp.mean(resid * resid, axis=-1, keepdims=True) + 1e-06)
    normed = (resid * factor).astype(jnp.bfloat16)
    pair = jnp.concatenate([normed, send(normed, SWAP_Z)], 0)
    rows = jnp.concatenate([pair] + [send(pair, shift1(s)) for s in (1, 2, 3)], 0)
    rows = [rows] + [send(rows, shift2(s)) for s in (1, 2, 3)]

    vec = jnp.concatenate(
        [enc_bias, thresh_levels.astype(jnp.float32) * 0.125, jnp.pad(dec_bias, ((0, 0), (0, 256 - width)))], 0
    )
    vec = jnp.pad(vec, ((0, 5), (0, 0)))
    vec_other = send(vec, SWAP_CORE)
    enc_own = enc_weight[0]
    enc_other = send(enc_own, SWAP_CORE)
    dec_own = dec_weight[0].reshape(layers * width, features)
    dec_other = fetch(send(dec_own, SWAP_CORE))

    acts = encode(info, rows, enc_own, enc_other, vec, vec_other)

    a0 = jnp.stack([acts, send(acts, SWAP_Z)])
    a1, a3, a2 = (send(a0, shift1(s)) for s in (1, 3, 2))
    l0, r0 = send(a0, shift2(1)), send(a0, shift2(3))
    h = jnp.concatenate([a1, a3], 0)
    rh, l2 = send(h, shift2(3)), send(a2, shift2(1))
    lh, r2 = send(h, shift2(1)), send(a2, shift2(3))
    far0 = send(l0, shift2(1))
    farh, far2 = send(rh, shift2(3)), send(l2, shift2(1))

    def at(s2, s1):
        return (s2 * 4 + s1) * 2

    w = (dec_own, dec_other)

    def step(*args, **kw):
        return decode(info, *args, **kw)

    (part,) = step([a0, a2, a1, a3], [at(0, 0), at(0, 2), at(0, 1), at(0, 3)], *w, None)
    (part,) = step([l0, r0, far0], [at(1, 0), at(3, 0), at(2, 0)], *w, part)

    def pieces(*named):
        out, offs = [], []
        for x, s2, s1 in named:
            if x.shape[0] == 2:
                out.append(x)
                offs.append(at(s2, s1))
            else:
                out.append(x)
                offs.append((at(s2, 1), at(s2, 3)))
        return out, offs

    (part,) = step(*pieces((rh, 3, None), (l2, 1, 2)), *w, part)
    (part,) = step(*pieces((lh, 1, None), (r2, 3, 2)), *w, part)
    part, sent = step(*pieces((farh, 2, None), (far2, 2, 2)), *w, part, last=True)

    part = part.reshape(2, layers, width, 256)
    total = lax.dynamic_index_in_dim(part, my_layer, 1, keepdims=False)
    got = lax.all_to_all(sent, "layer", 0, 0).astype(jnp.float32)
    for source in range(layers - 1):
        total = total + jnp.where(source < my_layer, got[source], 0.0)
    bias = jnp.stack([vec[2, :width], vec_other[2, :width]])[:, :, None]
    total = (total + bias).astype(jnp.bfloat16)

    theirs = send(total[1], SWAP_CORE)
    mine = total[0]
    first = info[0] == 0
    both = jnp.stack([jnp.where(first, mine, theirs), jnp.where(first, theirs, mine)])
    both = both.reshape(2, width, 32, 8).transpose(2, 0, 3, 1)
    return both.reshape(1, 512, width)


def solution(mesh):
    in_specs = (
        P("layer", "feat", None),
        P("layer", None, "feat"),
        P("layer", "feat"),
        P("layer", "feat"),
        P("layer", None, "feat", None),
        P("layer", "feat"),
    )
    out_specs = P("layer", None, "feat")
    return jax.shard_map(work, mesh=mesh, in_specs=in_specs, out_specs=out_specs, check_vma=False)
```

```python
import jax
import jax.numpy as jnp
import numpy as np
from jax import lax
from jax.experimental import pallas as pl
from jax.experimental.pallas import tpu as pltpu
from jax.sharding import PartitionSpec as P


NZ, NY, NX = 2, 4, 4


def place(z, y, x, c):
    return (z % NZ) * 32 + (y % NY) * 8 + (x % NX) * 2 + c


ALL = [(z, y, x, c) for z in range(NZ) for y in range(NY) for x in range(NX) for c in range(2)]


def along(c, first, second, z):
    return place(z, second, first, c) if c == 0 else place(z, first, second, c)


OWNERS = [
    [layer * 64 + place(z, y, x, c) for layer in range(4) for c in range(2)]
    for z in range(NZ)
    for y in range(NY)
    for x in range(NX)
]
SWAP_CORE = [(place(z, y, x, c), place(z, y, x, 1 - c)) for z, y, x, c in ALL]
SWAP_Z = [(place(z, y, x, c), place(1 - z, y, x, c)) for z, y, x, c in ALL]
RING = [(c, z, p, q) for c in range(2) for z in range(2) for p in range(4) for q in range(4)]


def shift1(s):
    return [(along(c, p, q, z), along(c, (p + s) % 4, q, z)) for c, z, p, q in RING]


def shift2(s):
    return [(along(c, p, q, z), along(c, p, (q + s) % 4, z)) for c, z, p, q in RING]


def table():
    rows = np.zeros((64, 40), np.int32)
    for z, y, x, c in ALL:
        p, q = (x, y) if c == 0 else (y, x)
        row = [c]
        for s2 in range(4):
            for s1 in range(4):
                for j in range(2):
                    p1, q2 = (p - s1) % 4, (q - s2) % 4
                    yy, xx = (q2, p1) if c == 0 else (p1, q2)
                    row.append((z ^ j) * 16 + yy * 4 + xx)
        rows[place(z, y, x, c), : len(row)] = row
    return rows


TABLE = table()
KSTEPS = 4
BLOCKS = [(s2, s1, j) for j in (0, 1) for s2 in (0, 1, 3, 2) for s1 in (0, 1, 3, 2)]


def at(s2, s1, j):
    return 1 + (s2 * 4 + s1) * 2 + j


def encode_body(info, *refs):
    xs, (w_own, w_other, vec_own, vec_other, out, acc) = refs[:-6], refs[-6:]
    kb = xs[0].shape[1] // KSTEPS
    rows = [jnp.concatenate([x[:, k * kb : k * kb + kb] for x in xs], 0) for k in range(KSTEPS)]
    for i, (w, vec) in enumerate(((w_own, vec_own), (w_other, vec_other))):
        pre = vec[0:1, :]
        for k, x in enumerate(rows):
            pre = pre + jnp.dot(x, w[k * kb : k * kb + kb, :], preferred_element_type=jnp.float32)
        acc[0] = pre * jnp.clip((pre - vec[1:2, :]) / 0.25, 0.0, 1.0)
        for b, source in enumerate(BLOCKS):
            row = pl.multiple_of(info[at(*source)] * 8, 8)
            acc[1, pl.ds(row, 8), :] = acc[0, b * 8 : b * 8 + 8, :]
        col = pl.multiple_of((info[0] ^ i) * 256, 256)
        out[:, pl.ds(col, 256)] = acc[1].astype(jnp.bfloat16)


def encode(info, xs, w_own, w_other, vec_own, vec_other):
    args = [pltpu.with_memory_space_constraint(v, pltpu.VMEM) for v in (*xs, w_own, w_other, vec_own, vec_other)]
    vmem = pl.BlockSpec(memory_space=pltpu.VMEM)
    return pl.pallas_call(
        encode_body,
        out_shape=jax.ShapeDtypeStruct((256, 512), jnp.bfloat16),
        in_specs=[pl.BlockSpec(memory_space=pltpu.SMEM)] + [vmem] * len(args),
        out_specs=vmem,
        scratch_shapes=[pltpu.VMEM((2, 256, 256), jnp.float32)],
        compiler_params=pltpu.CompilerParams(vmem_limit_bytes=20 << 20),
        name="encode",
    )(info, *args)


def decode(info, pieces, offsets, w_own, w_other, acc, last=False):
    n_in = len(pieces) + 2 + (acc is not None)

    def body(info, *refs):
        acts, (wo, wp) = refs[: len(pieces)], refs[len(pieces) : len(pieces) + 2]
        out = refs[n_in]
        for h, w in ((0, wo), (1, wp)):
            total = None if acc is None else refs[n_in - 1][h]
            for a, off in zip(acts, offsets):
                for i in range(a.shape[0]):
                    col = pl.multiple_of(info[at(*off[i])] * 512, 512)
                    part = lax.dot_general(
                        w[:, pl.ds(col, 512)], a[i], (((1,), (1,)), ((), ())), preferred_element_type=jnp.float32
                    )
                    total = part if total is None else total + part
            out[h] = total
            if last:
                sent = refs[n_in + 1]
                for e in range(4):
                    sent[e, info[0] ^ h] = out[h, e * 72 : e * 72 + 72, :].astype(jnp.bfloat16)

    vmem = pl.BlockSpec(memory_space=pltpu.VMEM)
    args = [*pieces, w_own, w_other] + ([] if acc is None else [acc])
    args = [pltpu.with_memory_space_constraint(v, pltpu.VMEM) for v in args]
    shapes = [jax.ShapeDtypeStruct((2, 288, 256), jnp.float32)]
    if last:
        shapes.append(jax.ShapeDtypeStruct((4, 2, 72, 256), jnp.bfloat16))
    return pl.pallas_call(
        body,
        out_shape=shapes,
        in_specs=[pl.BlockSpec(memory_space=pltpu.SMEM)] + [vmem] * len(args),
        out_specs=[vmem] * len(shapes),
        compiler_params=pltpu.CompilerParams(vmem_limit_bytes=16 << 20),
        name="decode",
    )(info, *args)


def finish_body(info, got, bias, out):
    token = lax.broadcasted_iota(jnp.int32, (256, 512), 1)
    held = lax.broadcasted_iota(jnp.int32, (256, 512), 0)
    result = None
    for c in range(2):
        total = bias[:, 0:1]
        for source in range(4):
            total = total + jnp.where(source <= info[0], got[source * 2 + c].astype(jnp.float32), 0.0)
        here = token == (held // 8 * 2 + c) * 8 + held % 8
        moved = jnp.dot(
            total.astype(jnp.bfloat16),
            jnp.where(here, 1.0, 0.0).astype(jnp.bfloat16),
            preferred_element_type=jnp.float32,
        )
        result = moved if result is None else result + moved
    out[...] = result.astype(jnp.bfloat16)


def finish(layer, got, bias):
    vmem = pl.BlockSpec(memory_space=pltpu.VMEM)
    return pl.pallas_call(
        finish_body,
        out_shape=jax.ShapeDtypeStruct((got.shape[1], 512), jnp.bfloat16),
        in_specs=[pl.BlockSpec(memory_space=pltpu.SMEM), vmem, vmem],
        out_specs=vmem,
        compiler_params=pltpu.CompilerParams(vmem_limit_bytes=8 << 20),
        name="finish",
    )(layer[None], got, bias)


def fetch(x):
    return pl.pallas_call(
        lambda src, dst: pltpu.sync_copy(src, dst),
        out_shape=jax.ShapeDtypeStruct(x.shape, x.dtype),
        in_specs=[pl.BlockSpec(memory_space=pl.ANY)],
        out_specs=pl.BlockSpec(memory_space=pltpu.VMEM),
        compiler_params=pltpu.CompilerParams(vmem_limit_bytes=16 << 20),
        name="fetch",
    )(x)


def work(residuals, enc_weight, enc_bias, thresh_levels, dec_weight, dec_bias):
    me, my_layer = lax.axis_index("feat"), lax.axis_index("layer")
    info = lax.dynamic_index_in_dim(jnp.asarray(TABLE), me, 0, keepdims=False)
    layers, width, features = dec_weight.shape[1:]

    def send(x, pairs):
        return lax.ppermute(x, "feat", pairs)

    def join(*xs):
        return jnp.concatenate(xs, 0)

    resid = residuals[0].astype(jnp.float32)
    factor = lax.rsqrt(jnp.mean(resid * resid, axis=-1, keepdims=True) + 1e-06)
    normed = (resid * factor).astype(jnp.bfloat16)
    nz = send(normed, SWAP_Z)
    m = join(*(send(normed, shift1(s)) for s in (1, 3, 2)))
    mz = send(m, SWAP_Z)
    p, q = join(normed, m), join(nz, mz)
    rows = [x for v in (p, q) for x in [v] + [send(v, shift2(s)) for s in (1, 3, 2)]]

    vec = jnp.pad(join(enc_bias, thresh_levels.astype(jnp.float32) * 0.125), ((0, 6), (0, 0)))
    vec_other = send(vec, SWAP_CORE)
    enc_own = enc_weight[0]
    enc_other = send(enc_own, SWAP_CORE)
    dec_own = dec_weight[0].reshape(layers * width, features)
    dec_other = fetch(send(dec_own, SWAP_CORE))

    acts = encode(info, rows, enc_own, enc_other, vec, vec_other)

    own = acts[None]
    a1, a3, z0, a2 = (
        send(own, to)
        for to in (shift1(1), shift1(3), SWAP_Z, shift1(2))
    )
    lo, ro = send(own, shift2(1)), send(own, shift2(3))
    z1, z3 = send(a1, SWAP_Z), send(a3, SWAP_Z)
    h = join(a1, a3)
    rh, lh = send(h, shift2(3)), send(h, shift2(1))
    b2 = send(z0, shift1(2))
    g = join(a2, z0)
    lg, rg = send(g, shift2(1)), send(g, shift2(3))
    farh = send(rh, shift2(3))
    k = join(z1, z3, b2)
    lk, rk = send(k, shift2(1)), send(k, shift2(3))
    faro, farg, fark = send(lo, shift2(1)), send(rg, shift2(3)), send(lk, shift2(1))

    o_at, h_at, g_at, k_at = ((0, 0),), ((1, 0), (3, 0)), ((2, 0), (0, 1)), ((1, 1), (3, 1), (2, 1))
    plan = (
        ((own, 0, o_at), (h, 0, h_at), (g, 0, g_at)),
        ((lo, 1, o_at), (ro, 3, o_at), (rh, 3, h_at), (lh, 1, h_at), (k, 0, k_at)),
        ((rg, 3, g_at), (lg, 1, g_at), (farh, 2, h_at), (faro, 2, o_at)),
        ((lk, 1, k_at), (rk, 3, k_at)),
        ((farg, 2, g_at), (fark, 2, k_at)),
    )
    part = None
    for n, group in enumerate(plan):
        part, *sent = decode(
            info,
            [x for x, _, _ in group],
            [[(s2, *w) for w in where] for _, s2, where in group],
            dec_own,
            dec_other,
            part,
            last=n == len(plan) - 1,
        )

    got = lax.all_to_all(sent[0].reshape(8, width, 256), ("layer", "feat"), 0, 0, axis_index_groups=OWNERS)
    bias = jnp.broadcast_to(dec_bias[0][:, None], (width, 128))
    return finish(my_layer, got, bias).T[None]


def solution(mesh):
    in_specs = (
        P("layer", "feat", None),
        P("layer", None, "feat"),
        P("layer", "feat"),
        P("layer", "feat"),
        P("layer", None, "feat", None),
        P("layer", "feat"),
    )
    out_specs = P("layer", None, "feat")
    return jax.shard_map(work, mesh=mesh, in_specs=in_specs, out_specs=out_specs, check_vma=False)
```

```python
import jax
import jax.numpy as jnp
import numpy as np
from jax import lax
from jax.experimental import pallas as pl
from jax.experimental.pallas import tpu as pltpu
from jax.sharding import PartitionSpec as P


NZ, NY, NX = 2, 4, 4


def place(z, y, x, c):
    return (z % NZ) * 32 + (y % NY) * 8 + (x % NX) * 2 + c


ALL = [(z, y, x, c) for z in range(NZ) for y in range(NY) for x in range(NX) for c in range(2)]


def along(c, first, second, z):
    return place(z, second, first, c) if c == 0 else place(z, first, second, c)


SWAP_CORE = [(place(z, y, x, c), place(z, y, x, 1 - c)) for z, y, x, c in ALL]
SWAP_Z = [(place(z, y, x, c), place(1 - z, y, x, c)) for z, y, x, c in ALL]
RING = [(c, z, p, q) for c in range(2) for z in range(2) for p in range(4) for q in range(4)]


def shift1(s):
    return [(along(c, p, q, z), along(c, (p + s) % 4, q, z)) for c, z, p, q in RING]


def shift2(s):
    return [(along(c, p, q, z), along(c, p, (q + s) % 4, z)) for c, z, p, q in RING]


def table():
    rows = np.zeros((64, 40), np.int32)
    for z, y, x, c in ALL:
        p, q = (x, y) if c == 0 else (y, x)
        row = [c]
        for s2 in range(4):
            for s1 in range(4):
                for j in range(2):
                    p1, q2 = (p - s1) % 4, (q - s2) % 4
                    yy, xx = (q2, p1) if c == 0 else (p1, q2)
                    row.append((z ^ j) * 16 + yy * 4 + xx)
        rows[place(z, y, x, c), : len(row)] = row
    return rows


TABLE = table()
KSTEPS = 4
BLOCKS = [(s2, s1, j) for j in (0, 1) for s2 in (0, 1, 3, 2) for s1 in (0, 1, 3, 2)]


def at(s2, s1, j):
    return 1 + (s2 * 4 + s1) * 2 + j


def encode_body(info, *refs):
    xs, (w_own, w_other, vec_own, vec_other, out, acc) = refs[:-6], refs[-6:]
    kb = xs[0].shape[1] // KSTEPS
    rows = [jnp.concatenate([x[:, k * kb : k * kb + kb] for x in xs], 0) for k in range(KSTEPS)]
    for i, (w, vec) in enumerate(((w_own, vec_own), (w_other, vec_other))):
        pre = vec[0:1, :]
        for k, x in enumerate(rows):
            pre = pre + jnp.dot(x, w[k * kb : k * kb + kb, :], preferred_element_type=jnp.float32)
        acc[0] = pre * jnp.clip((pre - vec[1:2, :]) / 0.25, 0.0, 1.0)
        for b, source in enumerate(BLOCKS):
            row = pl.multiple_of(info[at(*source)] * 8, 8)
            acc[1, pl.ds(row, 8), :] = acc[0, b * 8 : b * 8 + 8, :]
        col = pl.multiple_of((info[0] ^ i) * 256, 256)
        out[:, pl.ds(col, 256)] = acc[1].astype(jnp.bfloat16)


def encode(info, xs, w_own, w_other, vec_own, vec_other):
    args = [pltpu.with_memory_space_constraint(v, pltpu.VMEM) for v in (*xs, w_own, w_other, vec_own, vec_other)]
    vmem = pl.BlockSpec(memory_space=pltpu.VMEM)
    return pl.pallas_call(
        encode_body,
        out_shape=jax.ShapeDtypeStruct((256, 512), jnp.bfloat16),
        in_specs=[pl.BlockSpec(memory_space=pltpu.SMEM)] + [vmem] * len(args),
        out_specs=vmem,
        scratch_shapes=[pltpu.VMEM((2, 256, 256), jnp.float32)],
        compiler_params=pltpu.CompilerParams(vmem_limit_bytes=20 << 20),
        name="encode",
    )(info, *args)


def decode(info, pieces, offsets, w_own, w_other, acc, last=False):
    n_in = len(pieces) + 2 + (acc is not None)

    def body(info, *refs):
        acts, (wo, wp) = refs[: len(pieces)], refs[len(pieces) : len(pieces) + 2]
        out = refs[n_in]
        for h, w in ((0, wo), (1, wp)):
            total = None if acc is None else refs[n_in - 1][h]
            for a, off in zip(acts, offsets):
                for i in range(a.shape[0]):
                    col = pl.multiple_of(info[at(*off[i])] * 512, 512)
                    part = lax.dot_general(
                        w[:, pl.ds(col, 512)], a[i], (((1,), (1,)), ((), ())), preferred_element_type=jnp.float32
                    )
                    total = part if total is None else total + part
            out[h] = total
        if last:
            layer = info[39]
            for k, ref in enumerate(refs[n_in + 1 :]):
                for h in range(2):
                    row = pl.multiple_of(jnp.minimum(layer + k, 3) * 72, 8)
                    ref[h] = out[h, pl.ds(row, 72), :].astype(ref.dtype)

    vmem = pl.BlockSpec(memory_space=pltpu.VMEM)
    args = [*pieces, w_own, w_other] + ([] if acc is None else [acc])
    args = [pltpu.with_memory_space_constraint(v, pltpu.VMEM) for v in args]
    shapes = [jax.ShapeDtypeStruct((2, 288, 256), jnp.float32)]
    if last:
        shapes += [jax.ShapeDtypeStruct((2, 72, 256), jnp.bfloat16 if k else jnp.float32) for k in range(4)]
    return pl.pallas_call(
        body,
        out_shape=shapes,
        in_specs=[pl.BlockSpec(memory_space=pltpu.SMEM)] + [vmem] * len(args),
        out_specs=[vmem] * len(shapes),
        compiler_params=pltpu.CompilerParams(vmem_limit_bytes=16 << 20),
        name="decode",
    )(info, *args)


def total_body(own, one, two, three, bias, mine, theirs):
    for h, out in ((0, mine), (1, theirs)):
        total = own[h] + one[h].astype(jnp.float32) + two[h].astype(jnp.float32) + three[h].astype(jnp.float32)
        out[...] = (total + bias[h][:, 0:1]).astype(jnp.bfloat16)


def sum_up(own, earlier, bias):
    vmem = pl.BlockSpec(memory_space=pltpu.VMEM)
    return pl.pallas_call(
        total_body,
        out_shape=[jax.ShapeDtypeStruct(own.shape[1:], jnp.bfloat16)] * 2,
        in_specs=[vmem] * 5,
        out_specs=[vmem] * 2,
        compiler_params=pltpu.CompilerParams(vmem_limit_bytes=8 << 20),
        name="sum_up",
    )(own, *earlier, bias)


def finish_body(info, mine, theirs, out):
    token = lax.broadcasted_iota(jnp.int32, (256, 512), 1)
    held = lax.broadcasted_iota(jnp.int32, (256, 512), 0)
    result = None
    for i, total in enumerate((mine, theirs)):
        here = token == (held // 8 * 2 + (info[0] ^ i)) * 8 + held % 8
        moved = jnp.dot(
            total[...], jnp.where(here, 1.0, 0.0).astype(jnp.bfloat16), preferred_element_type=jnp.float32
        )
        result = moved if result is None else result + moved
    out[...] = result.astype(jnp.bfloat16)


def finish(info, mine, theirs):
    vmem = pl.BlockSpec(memory_space=pltpu.VMEM)
    return pl.pallas_call(
        finish_body,
        out_shape=jax.ShapeDtypeStruct((mine.shape[0], 512), jnp.bfloat16),
        in_specs=[pl.BlockSpec(memory_space=pltpu.SMEM), vmem, vmem],
        out_specs=vmem,
        compiler_params=pltpu.CompilerParams(vmem_limit_bytes=8 << 20),
        name="finish",
    )(info, mine, theirs)


def fetch(x):
    return pl.pallas_call(
        lambda src, dst: pltpu.sync_copy(src, dst),
        out_shape=jax.ShapeDtypeStruct(x.shape, x.dtype),
        in_specs=[pl.BlockSpec(memory_space=pl.ANY)],
        out_specs=pl.BlockSpec(memory_space=pltpu.VMEM),
        compiler_params=pltpu.CompilerParams(vmem_limit_bytes=16 << 20),
        name="fetch",
    )(x)


def work(residuals, enc_weight, enc_bias, thresh_levels, dec_weight, dec_bias):
    me, my_layer = lax.axis_index("feat"), lax.axis_index("layer")
    info = lax.dynamic_index_in_dim(jnp.asarray(TABLE), me, 0, keepdims=False).at[39].set(my_layer)
    layers, width, features = dec_weight.shape[1:]

    def send(x, pairs):
        return lax.ppermute(x, "feat", pairs)

    def join(*xs):
        return jnp.concatenate(xs, 0)

    resid = residuals[0].astype(jnp.float32)
    factor = lax.rsqrt(jnp.mean(resid * resid, axis=-1, keepdims=True) + 1e-06)
    normed = (resid * factor).astype(jnp.bfloat16)
    nz = send(normed, SWAP_Z)
    m = join(*(send(normed, shift1(s)) for s in (1, 3, 2)))
    mz = send(m, SWAP_Z)
    p, q = join(normed, m), join(nz, mz)
    rows = [x for v in (p, q) for x in [v] + [send(v, shift2(s)) for s in (1, 3, 2)]]

    wide_bias = jnp.pad(dec_bias, ((0, 0), (0, 256 - width)))
    vec = jnp.pad(join(enc_bias, thresh_levels.astype(jnp.float32) * 0.125, wide_bias), ((0, 5), (0, 0)))
    vec_other = send(vec, SWAP_CORE)
    enc_own = enc_weight[0]
    enc_other = send(enc_own, SWAP_CORE)
    dec_own = dec_weight[0].reshape(layers * width, features)
    dec_other = fetch(send(dec_own, SWAP_CORE))

    acts = encode(info, rows, enc_own, enc_other, vec, vec_other)

    own = acts[None]
    a1, a3, z0, a2 = (
        send(own, to)
        for to in (shift1(1), shift1(3), SWAP_Z, shift1(2))
    )
    lo, ro = send(own, shift2(1)), send(own, shift2(3))
    z1, z3 = send(a1, SWAP_Z), send(a3, SWAP_Z)
    h = join(a1, a3)
    rh, lh = send(h, shift2(3)), send(h, shift2(1))
    b2 = send(z0, shift1(2))
    g = join(a2, z0)
    lg, rg = send(g, shift2(1)), send(g, shift2(3))
    farh = send(rh, shift2(3))
    k = join(z1, z3, b2)
    lk, rk = send(k, shift2(1)), send(k, shift2(3))
    faro, farg, fark = send(lo, shift2(1)), send(rg, shift2(3)), send(lk, shift2(1))

    o_at, h_at, g_at, k_at = ((0, 0),), ((1, 0), (3, 0)), ((2, 0), (0, 1)), ((1, 1), (3, 1), (2, 1))
    plan = (
        ((own, 0, o_at), (h, 0, h_at), (g, 0, g_at)),
        ((lo, 1, o_at), (ro, 3, o_at), (rh, 3, h_at), (lh, 1, h_at), (k, 0, k_at)),
        ((rg, 3, g_at), (lg, 1, g_at), (farh, 2, h_at), (faro, 2, o_at)),
        ((lk, 1, k_at), (rk, 3, k_at)),
        ((farg, 2, g_at), (fark, 2, k_at)),
    )
    part = None
    for n, group in enumerate(plan):
        part, *sent = decode(
            info,
            [x for x, _, _ in group],
            [[(s2, *w) for w in where] for _, s2, where in group],
            dec_own,
            dec_other,
            part,
            last=n == len(plan) - 1,
        )

    own_part, *later = sent
    earlier = []
    for k, x in enumerate(later, 1):
        earlier.append(lax.ppermute(x, "layer", [(n, n + k) for n in range(layers - k)]))
    bias = jnp.stack([vec[2, :width], vec_other[2, :width]])
    bias = jnp.broadcast_to(bias[:, :, None], (2, width, 128))
    mine, theirs = sum_up(own_part, earlier, bias)

    return finish(info, mine, send(theirs, SWAP_CORE)).T[None]


def solution(mesh):
    in_specs = (
        P("layer", "feat", None),
        P("layer", None, "feat"),
        P("layer", "feat"),
        P("layer", "feat"),
        P("layer", None, "feat", None),
        P("layer", "feat"),
    )
    out_specs = P("layer", None, "feat")
    return jax.shard_map(work, mesh=mesh, in_specs=in_specs, out_specs=out_specs, check_vma=False)
```

```python
import jax
import jax.numpy as jnp
import numpy as np
from jax import lax
from jax.experimental import pallas as pl
from jax.experimental.pallas import tpu as pltpu
from jax.sharding import PartitionSpec as P


NZ, NY, NX = 2, 4, 4


def place(z, y, x, c):
    return (z % NZ) * 32 + (y % NY) * 8 + (x % NX) * 2 + c


ALL = [(z, y, x, c) for z in range(NZ) for y in range(NY) for x in range(NX) for c in range(2)]


def along(c, first, second, z):
    return place(z, second, first, c) if c == 0 else place(z, first, second, c)


SWAP_CORE = [(place(z, y, x, c), place(z, y, x, 1 - c)) for z, y, x, c in ALL]
SWAP_Z = [(place(z, y, x, c), place(1 - z, y, x, c)) for z, y, x, c in ALL]
RING = [(c, z, p, q) for c in range(2) for z in range(2) for p in range(4) for q in range(4)]


def shift1(s):
    return [(along(c, p, q, z), along(c, (p + s) % 4, q, z)) for c, z, p, q in RING]


def shift2(s):
    return [(along(c, p, q, z), along(c, p, (q + s) % 4, z)) for c, z, p, q in RING]


def table():
    rows = np.zeros((64, 40), np.int32)
    for z, y, x, c in ALL:
        p, q = (x, y) if c == 0 else (y, x)
        row = [c]
        for s2 in range(4):
            for s1 in range(4):
                for j in range(2):
                    p1, q2 = (p - s1) % 4, (q - s2) % 4
                    yy, xx = (q2, p1) if c == 0 else (p1, q2)
                    row.append((z ^ j) * 16 + yy * 4 + xx)
        rows[place(z, y, x, c), : len(row)] = row
    return rows


TABLE = table()
KSTEPS = 4
BLOCKS = [(s2, s1, j) for j in (0, 1) for s2 in (0, 1, 3, 2) for s1 in (0, 1, 3, 2)]


def at(s2, s1, j):
    return 1 + (s2 * 4 + s1) * 2 + j


def encode_body(info, *refs):
    xs, (w_own, w_other, vec_own, vec_other, out, acc) = refs[:-6], refs[-6:]
    kb = xs[0].shape[1] // KSTEPS
    rows = [jnp.concatenate([x[:, k * kb : k * kb + kb] for x in xs], 0) for k in range(KSTEPS)]
    for i, (w, vec) in enumerate(((w_own, vec_own), (w_other, vec_other))):
        pre = vec[0:1, :]
        for k, x in enumerate(rows):
            pre = pre + jnp.dot(x, w[k * kb : k * kb + kb, :], preferred_element_type=jnp.float32)
        acc[0] = pre * jnp.clip((pre - vec[1:2, :]) / 0.25, 0.0, 1.0)
        for b, source in enumerate(BLOCKS):
            row = pl.multiple_of(info[at(*source)] * 8, 8)
            acc[1, pl.ds(row, 8), :] = acc[0, b * 8 : b * 8 + 8, :]
        col = pl.multiple_of((info[0] ^ i) * 256, 256)
        out[:, pl.ds(col, 256)] = acc[1].astype(jnp.bfloat16)


def encode(info, xs, w_own, w_other, vec_own, vec_other):
    args = [pltpu.with_memory_space_constraint(v, pltpu.VMEM) for v in (*xs, w_own, w_other, vec_own, vec_other)]
    vmem = pl.BlockSpec(memory_space=pltpu.VMEM)
    return pl.pallas_call(
        encode_body,
        out_shape=jax.ShapeDtypeStruct((256, 512), jnp.bfloat16),
        in_specs=[pl.BlockSpec(memory_space=pltpu.SMEM)] + [vmem] * len(args),
        out_specs=vmem,
        scratch_shapes=[pltpu.VMEM((2, 256, 256), jnp.float32)],
        compiler_params=pltpu.CompilerParams(vmem_limit_bytes=20 << 20),
        name="encode",
    )(info, *args)


def decode(info, pieces, offsets, w_own, w_other, acc, last=False):
    n_in = len(pieces) + 2 + (acc is not None)

    def body(info, *refs):
        acts, (wo, wp) = refs[: len(pieces)], refs[len(pieces) : len(pieces) + 2]
        out = refs[n_in]
        for h, w in ((0, wo), (1, wp)):
            total = None if acc is None else refs[n_in - 1][h]
            for a, off in zip(acts, offsets):
                for i in range(a.shape[0]):
                    col = pl.multiple_of(info[at(*off[i])] * 512, 512)
                    part = lax.dot_general(
                        w[:, pl.ds(col, 512)], a[i], (((1,), (1,)), ((), ())), preferred_element_type=jnp.float32
                    )
                    total = part if total is None else total + part
            out[h] = total
        if last:
            layer = info[39]
            for k, ref in enumerate(refs[n_in + 1 :]):
                for h in range(2):
                    row = pl.multiple_of(jnp.minimum(layer + k, 3) * 72, 8)
                    ref[h] = out[h, pl.ds(row, 72), :].astype(ref.dtype)

    vmem = pl.BlockSpec(memory_space=pltpu.VMEM)
    args = [*pieces, w_own, w_other] + ([] if acc is None else [acc])
    args = [pltpu.with_memory_space_constraint(v, pltpu.VMEM) for v in args]
    shapes = [jax.ShapeDtypeStruct((2, 288, 256), jnp.float32)]
    if last:
        shapes += [jax.ShapeDtypeStruct((2, 72, 256), jnp.bfloat16 if k else jnp.float32) for k in range(4)]
    return pl.pallas_call(
        body,
        out_shape=shapes,
        in_specs=[pl.BlockSpec(memory_space=pltpu.SMEM)] + [vmem] * len(args),
        out_specs=[vmem] * len(shapes),
        compiler_params=pltpu.CompilerParams(vmem_limit_bytes=16 << 20),
        name="decode",
    )(info, *args)


def total_body(own, one, two, three, bias, mine, theirs):
    for h, out in ((0, mine), (1, theirs)):
        total = own[h] + one[h].astype(jnp.float32) + two[h].astype(jnp.float32) + three[h].astype(jnp.float32)
        out[...] = (total + bias[h][:, 0:1]).astype(jnp.bfloat16)


def sum_up(own, earlier, bias):
    vmem = pl.BlockSpec(memory_space=pltpu.VMEM)
    return pl.pallas_call(
        total_body,
        out_shape=[jax.ShapeDtypeStruct(own.shape[1:], jnp.bfloat16)] * 2,
        in_specs=[vmem] * 5,
        out_specs=[vmem] * 2,
        compiler_params=pltpu.CompilerParams(vmem_limit_bytes=8 << 20),
        name="sum_up",
    )(own, *earlier, bias)


def finish_body(move, mine, theirs, out):
    moved = jnp.dot(mine[...], move[0], preferred_element_type=jnp.float32)
    out[...] = (moved + jnp.dot(theirs[...], move[1], preferred_element_type=jnp.float32)).astype(jnp.bfloat16)


def finish(move, mine, theirs):
    vmem = pl.BlockSpec(memory_space=pltpu.VMEM)
    return pl.pallas_call(
        finish_body,
        out_shape=jax.ShapeDtypeStruct((mine.shape[0], 512), jnp.bfloat16),
        in_specs=[vmem] * 3,
        out_specs=vmem,
        compiler_params=pltpu.CompilerParams(vmem_limit_bytes=8 << 20),
        name="finish",
    )(move, mine, theirs)


def fetch_body(info, src, dst, move):
    pltpu.sync_copy(src, dst)
    held, token = (lax.broadcasted_iota(jnp.int32, (256, 512), d) for d in (0, 1))
    for i in range(2):
        here = token == (held // 8 * 2 + (info[0] ^ i)) * 8 + held % 8
        move[i] = jnp.where(here, 1.0, 0.0).astype(jnp.bfloat16)


def fetch(info, x):
    return pl.pallas_call(
        fetch_body,
        out_shape=[jax.ShapeDtypeStruct(x.shape, x.dtype), jax.ShapeDtypeStruct((2, 256, 512), jnp.bfloat16)],
        in_specs=[pl.BlockSpec(memory_space=pltpu.SMEM), pl.BlockSpec(memory_space=pl.ANY)],
        out_specs=[pl.BlockSpec(memory_space=pltpu.VMEM)] * 2,
        compiler_params=pltpu.CompilerParams(vmem_limit_bytes=16 << 20),
        name="fetch",
    )(info, x)


def work(residuals, enc_weight, enc_bias, thresh_levels, dec_weight, dec_bias):
    me, my_layer = lax.axis_index("feat"), lax.axis_index("layer")
    info = lax.dynamic_index_in_dim(jnp.asarray(TABLE), me, 0, keepdims=False).at[39].set(my_layer)
    layers, width, features = dec_weight.shape[1:]

    def send(x, pairs):
        return lax.ppermute(x, "feat", pairs)

    def join(*xs):
        return jnp.concatenate(xs, 0)

    resid = residuals[0].astype(jnp.float32)
    factor = lax.rsqrt(jnp.mean(resid * resid, axis=-1, keepdims=True) + 1e-06)
    normed = (resid * factor).astype(jnp.bfloat16)
    nz = send(normed, SWAP_Z)
    m = join(*(send(normed, shift1(s)) for s in (1, 3, 2)))
    mz = send(m, SWAP_Z)
    p, q = join(normed, m), join(nz, mz)
    rows = [x for v in (p, q) for x in [v] + [send(v, shift2(s)) for s in (1, 3, 2)]]

    wide_bias = jnp.pad(dec_bias, ((0, 0), (0, 256 - width)))
    vec = jnp.pad(join(enc_bias, thresh_levels.astype(jnp.float32) * 0.125, wide_bias), ((0, 5), (0, 0)))
    vec_other = send(vec, SWAP_CORE)
    enc_own = enc_weight[0]
    enc_other = send(enc_own, SWAP_CORE)
    dec_own = dec_weight[0].reshape(layers * width, features)
    dec_other, move = fetch(info, send(dec_own, SWAP_CORE))

    acts = encode(info, rows, enc_own, enc_other, vec, vec_other)

    own = acts[None]
    a1, a3, z0, a2 = (
        send(own, to)
        for to in (shift1(1), shift1(3), SWAP_Z, shift1(2))
    )
    lo, ro = send(own, shift2(1)), send(own, shift2(3))
    z1, z3 = send(a1, SWAP_Z), send(a3, SWAP_Z)
    h = join(a1, a3)
    rh, lh = send(h, shift2(3)), send(h, shift2(1))
    b2 = send(z0, shift1(2))
    g = join(a2, z0)
    lg, rg = send(g, shift2(1)), send(g, shift2(3))
    farh = send(rh, shift2(3))
    k = join(z1, z3)
    lk, rk = send(k, shift2(1)), send(k, shift2(3))
    lb, rb = send(b2, shift2(1)), send(b2, shift2(3))
    faro, farg = send(lo, shift2(1)), send(rg, shift2(3))
    fark, farb = send(lk, shift2(1)), send(lb, shift2(1))

    o_at, h_at, g_at, k_at, b_at = ((0, 0),), ((1, 0), (3, 0)), ((2, 0), (0, 1)), ((1, 1), (3, 1)), ((2, 1),)
    plan = (
        ((own, 0, o_at), (h, 0, h_at), (g, 0, g_at), (k, 0, k_at), (b2, 0, b_at)),
        ((lo, 1, o_at), (ro, 3, o_at), (rh, 3, h_at), (lh, 1, h_at), (rg, 3, g_at)),
        ((lg, 1, g_at), (farh, 2, h_at), (faro, 2, o_at), (lk, 1, k_at)),
        ((rk, 3, k_at), (lb, 1, b_at), (rb, 3, b_at)),
        ((farg, 2, g_at), (fark, 2, k_at), (farb, 2, b_at)),
    )
    bias = jnp.stack([vec[2, :width], vec_other[2, :width]])
    bias = jnp.broadcast_to(bias[:, :, None], (2, width, 128))

    part = None
    for n, group in enumerate(plan):
        if n == 3:
            part, bias = lax.optimization_barrier((part, bias))
        part, *sent = decode(
            info,
            [x for x, _, _ in group],
            [[(s2, *w) for w in where] for _, s2, where in group],
            dec_own,
            dec_other,
            part,
            last=n == len(plan) - 1,
        )

    own_part, *later = sent
    earlier = []
    for k, x in enumerate(later, 1):
        earlier.append(lax.ppermute(x, "layer", [(n, n + k) for n in range(layers - k)]))
    mine, theirs = sum_up(own_part, earlier, bias)

    return finish(move, mine, send(theirs, SWAP_CORE)).T[None]


def solution(mesh):
    in_specs = (
        P("layer", "feat", None),
        P("layer", None, "feat"),
        P("layer", "feat"),
        P("layer", "feat"),
        P("layer", None, "feat", None),
        P("layer", "feat"),
    )
    out_specs = P("layer", None, "feat")
    return jax.shard_map(work, mesh=mesh, in_specs=in_specs, out_specs=out_specs, check_vma=False)
```

```python
import jax
import jax.numpy as jnp
import numpy as np
from jax import lax
from jax.experimental import pallas as pl
from jax.experimental.pallas import tpu as pltpu
from jax.sharding import PartitionSpec as P


NZ, NY, NX = 2, 4, 4


def place(z, y, x, c):
    return (z % NZ) * 32 + (y % NY) * 8 + (x % NX) * 2 + c


ALL = [(z, y, x, c) for z in range(NZ) for y in range(NY) for x in range(NX) for c in range(2)]


def along(c, first, second, z):
    return place(z, second, first, c) if c == 0 else place(z, first, second, c)


SWAP_CORE = [(place(z, y, x, c), place(z, y, x, 1 - c)) for z, y, x, c in ALL]
SWAP_Z = [(place(z, y, x, c), place(1 - z, y, x, c)) for z, y, x, c in ALL]
RING = [(c, z, p, q) for c in range(2) for z in range(2) for p in range(4) for q in range(4)]


def shift1(s):
    return [(along(c, p, q, z), along(c, (p + s) % 4, q, z)) for c, z, p, q in RING]


def shift2(s):
    return [(along(c, p, q, z), along(c, p, (q + s) % 4, z)) for c, z, p, q in RING]


def table():
    rows = np.zeros((64, 40), np.int32)
    for z, y, x, c in ALL:
        p, q = (x, y) if c == 0 else (y, x)
        row = [c]
        for s2 in range(4):
            for s1 in range(4):
                for j in range(2):
                    p1, q2 = (p - s1) % 4, (q - s2) % 4
                    yy, xx = (q2, p1) if c == 0 else (p1, q2)
                    row.append((z ^ j) * 16 + yy * 4 + xx)
        rows[place(z, y, x, c), : len(row)] = row
    return rows


TABLE = table()
KSTEPS = 4
BLOCKS = [(s2, s1, j) for j in (0, 1) for s2 in (0, 1, 3, 2) for s1 in (0, 1, 3, 2)]


def at(s2, s1, j):
    return 1 + (s2 * 4 + s1) * 2 + j


def encode_body(info, *refs):
    xs, (w_own, w_other, vec_own, vec_other, out, acc) = refs[:-6], refs[-6:]
    kb = xs[0].shape[1] // KSTEPS
    rows = [jnp.concatenate([x[:, k * kb : k * kb + kb] for x in xs], 0) for k in range(KSTEPS)]
    for i, (w, vec) in enumerate(((w_own, vec_own), (w_other, vec_other))):
        pre = vec[0:1, :]
        for k, x in enumerate(rows):
            pre = pre + jnp.dot(x, w[k * kb : k * kb + kb, :], preferred_element_type=jnp.float32)
        acc[0] = pre * jnp.clip((pre - vec[1:2, :]) / 0.25, 0.0, 1.0)
        for b, source in enumerate(BLOCKS):
            row = pl.multiple_of(info[at(*source)] * 8, 8)
            acc[1, pl.ds(row, 8), :] = acc[0, b * 8 : b * 8 + 8, :]
        col = pl.multiple_of((info[0] ^ i) * 256, 256)
        out[:, pl.ds(col, 256)] = acc[1].astype(jnp.bfloat16)


def encode(info, xs, w_own, w_other, vec_own, vec_other):
    args = [pltpu.with_memory_space_constraint(v, pltpu.VMEM) for v in (*xs, w_own, w_other, vec_own, vec_other)]
    vmem = pl.BlockSpec(memory_space=pltpu.VMEM)
    return pl.pallas_call(
        encode_body,
        out_shape=jax.ShapeDtypeStruct((256, 512), jnp.bfloat16),
        in_specs=[pl.BlockSpec(memory_space=pltpu.SMEM)] + [vmem] * len(args),
        out_specs=vmem,
        scratch_shapes=[pltpu.VMEM((2, 256, 256), jnp.float32)],
        compiler_params=pltpu.CompilerParams(vmem_limit_bytes=8 << 20),
        name="encode",
    )(info, *args)


def decode(info, pieces, offsets, w_own, w_other, acc, last=False):
    n_in = len(pieces) + 2 + (acc is not None)

    def body(info, *refs):
        acts, (wo, wp) = refs[: len(pieces)], refs[len(pieces) : len(pieces) + 2]
        out = refs[n_in]
        for h, w in ((0, wo), (1, wp)):
            total = None if acc is None else refs[n_in - 1][h]
            for a, off in zip(acts, offsets):
                for i in range(a.shape[0]):
                    col = pl.multiple_of(info[at(*off[i])] * 512, 512)
                    part = lax.dot_general(
                        w[:, pl.ds(col, 512)], a[i], (((1,), (1,)), ((), ())), preferred_element_type=jnp.float32
                    )
                    total = part if total is None else total + part
            out[h] = total
        if last:
            layer = info[39]
            for k, ref in enumerate(refs[n_in + 1 :]):
                for h in range(2):
                    row = pl.multiple_of(jnp.minimum(layer + k, 3) * 72, 8)
                    ref[h] = out[h, pl.ds(row, 72), :].astype(ref.dtype)

    vmem = pl.BlockSpec(memory_space=pltpu.VMEM)
    args = [*pieces, w_own, w_other] + ([] if acc is None else [acc])
    args = [pltpu.with_memory_space_constraint(v, pltpu.VMEM) for v in args]
    shapes = [jax.ShapeDtypeStruct((2, 288, 256), jnp.float32)]
    if last:
        shapes += [jax.ShapeDtypeStruct((2, 72, 256), jnp.bfloat16 if k else jnp.float32) for k in range(4)]
    return pl.pallas_call(
        body,
        out_shape=shapes,
        in_specs=[pl.BlockSpec(memory_space=pltpu.SMEM)] + [vmem] * len(args),
        out_specs=[vmem] * len(shapes),
        compiler_params=pltpu.CompilerParams(vmem_limit_bytes=8 << 20),
        name="decode",
    )(info, *args)


def total_body(own, one, two, three, bias, mine, theirs):
    for h, out in ((0, mine), (1, theirs)):
        total = own[h] + one[h].astype(jnp.float32) + two[h].astype(jnp.float32) + three[h].astype(jnp.float32)
        out[...] = (total + bias[h][:, 0:1]).astype(jnp.bfloat16)


def sum_up(own, earlier, bias):
    vmem = pl.BlockSpec(memory_space=pltpu.VMEM)
    return pl.pallas_call(
        total_body,
        out_shape=[jax.ShapeDtypeStruct(own.shape[1:], jnp.bfloat16)] * 2,
        in_specs=[vmem] * 5,
        out_specs=[vmem] * 2,
        compiler_params=pltpu.CompilerParams(vmem_limit_bytes=4 << 20),
        name="sum_up",
    )(own, *earlier, bias)


def finish_body(move, mine, theirs, out):
    moved = jnp.dot(mine[...], move[0], preferred_element_type=jnp.float32)
    out[...] = (moved + jnp.dot(theirs[...], move[1], preferred_element_type=jnp.float32)).astype(jnp.bfloat16)


def finish(move, mine, theirs):
    vmem = pl.BlockSpec(memory_space=pltpu.VMEM)
    return pl.pallas_call(
        finish_body,
        out_shape=jax.ShapeDtypeStruct((mine.shape[0], 512), jnp.bfloat16),
        in_specs=[vmem] * 3,
        out_specs=vmem,
        compiler_params=pltpu.CompilerParams(vmem_limit_bytes=4 << 20),
        name="finish",
    )(move, mine, theirs)


def fetch_body(info, src, dst, move):
    pltpu.sync_copy(src, dst)
    held, token = (lax.broadcasted_iota(jnp.int32, (256, 512), d) for d in (0, 1))
    for i in range(2):
        here = token == (held // 8 * 2 + (info[0] ^ i)) * 8 + held % 8
        move[i] = jnp.where(here, 1.0, 0.0).astype(jnp.bfloat16)


def fetch(info, x):
    return pl.pallas_call(
        fetch_body,
        out_shape=[jax.ShapeDtypeStruct(x.shape, x.dtype), jax.ShapeDtypeStruct((2, 256, 512), jnp.bfloat16)],
        in_specs=[pl.BlockSpec(memory_space=pltpu.SMEM), pl.BlockSpec(memory_space=pl.ANY)],
        out_specs=[pl.BlockSpec(memory_space=pltpu.VMEM)] * 2,
        compiler_params=pltpu.CompilerParams(vmem_limit_bytes=4 << 20),
        name="fetch",
    )(info, x)


def work(residuals, enc_weight, enc_bias, thresh_levels, dec_weight, dec_bias):
    me, my_layer = lax.axis_index("feat"), lax.axis_index("layer")
    info = lax.dynamic_index_in_dim(jnp.asarray(TABLE), me, 0, keepdims=False).at[39].set(my_layer)
    layers, width, features = dec_weight.shape[1:]

    def send(x, pairs):
        return lax.ppermute(x, "feat", pairs)

    def join(*xs):
        return jnp.concatenate(xs, 0)

    resid = residuals[0].astype(jnp.float32)
    factor = lax.rsqrt(jnp.mean(resid * resid, axis=-1, keepdims=True) + 1e-06)
    normed = (resid * factor).astype(jnp.bfloat16)
    nz = send(normed, SWAP_Z)
    m = join(*(send(normed, shift1(s)) for s in (1, 3, 2)))
    mz = send(m, SWAP_Z)
    p, q = join(normed, m), join(nz, mz)
    rows = [x for v in (p, q) for x in [v] + [send(v, shift2(s)) for s in (1, 3, 2)]]

    wide_bias = jnp.pad(dec_bias, ((0, 0), (0, 256 - width)))
    vec = jnp.pad(join(enc_bias, thresh_levels.astype(jnp.float32) * 0.125, wide_bias), ((0, 5), (0, 0)))
    vec_other = send(vec, SWAP_CORE)
    enc_own = enc_weight[0]
    enc_other = send(enc_own, SWAP_CORE)
    dec_own = dec_weight[0].reshape(layers * width, features)
    dec_other, move = fetch(info, send(dec_own, SWAP_CORE))

    acts = encode(info, rows, enc_own, enc_other, vec, vec_other)

    own = acts[None]
    a1, a3, z0, a2 = (
        send(own, to)
        for to in (shift1(1), shift1(3), SWAP_Z, shift1(2))
    )
    lo, ro = send(own, shift2(1)), send(own, shift2(3))
    z1, z3 = send(a1, SWAP_Z), send(a3, SWAP_Z)
    h = join(a1, a3)
    rh, lh = send(h, shift2(3)), send(h, shift2(1))
    g = join(a2, z0)
    lg, rg = send(g, shift2(1)), send(g, shift2(3))
    za2, zl, zr = (send(x, SWAP_Z) for x in (a2, lg[:1], rg[:1]))
    farh = send(rh, shift2(3))
    k = join(z1, z3)
    lk, rk = send(k, shift2(1)), send(k, shift2(3))
    faro, farg = send(lo, shift2(1)), send(rg, shift2(3))
    fark, farb = send(lk, shift2(1)), send(zl, shift2(1))

    o_at, h_at, g_at, k_at, b_at = ((0, 0),), ((1, 0), (3, 0)), ((2, 0), (0, 1)), ((1, 1), (3, 1)), ((2, 1),)
    plan = (
        ((own, 0, o_at), (h, 0, h_at), (g, 0, g_at), (k, 0, k_at), (za2, 0, b_at)),
        ((lo, 1, o_at), (ro, 3, o_at), (rh, 3, h_at), (lh, 1, h_at), (rg, 3, g_at)),
        ((lg, 1, g_at), (farh, 2, h_at), (faro, 2, o_at), (lk, 1, k_at), (zl, 1, b_at)),
        ((rk, 3, k_at), (zr, 3, b_at)),
        ((farg, 2, g_at), (fark, 2, k_at), (farb, 2, b_at)),
    )
    bias = jnp.stack([vec[2, :width], vec_other[2, :width]])
    bias = jnp.broadcast_to(bias[:, :, None], (2, width, 128))

    part = None
    for n, group in enumerate(plan):
        if n == 3:
            part, bias = lax.optimization_barrier((part, bias))
        part, *sent = decode(
            info,
            [x for x, _, _ in group],
            [[(s2, *w) for w in where] for _, s2, where in group],
            dec_own,
            dec_other,
            part,
            last=n == len(plan) - 1,
        )

    own_part, *later = sent
    earlier = []
    for k, x in enumerate(later, 1):
        earlier.append(lax.ppermute(x, "layer", [(n, n + k) for n in range(layers - k)]))
    mine, theirs = sum_up(own_part, earlier, bias)

    return finish(move, mine, send(theirs, SWAP_CORE)).T[None]


def solution(mesh):
    in_specs = (
        P("layer", "feat", None),
        P("layer", None, "feat"),
        P("layer", "feat"),
        P("layer", "feat"),
        P("layer", None, "feat", None),
        P("layer", "feat"),
    )
    out_specs = P("layer", None, "feat")
    return jax.shard_map(work, mesh=mesh, in_specs=in_specs, out_specs=out_specs, check_vma=False)
```

```python
import jax
import jax.numpy as jnp
import numpy as np
from jax import lax
from jax.experimental import pallas as pl
from jax.experimental.pallas import tpu as pltpu
from jax.sharding import PartitionSpec as P


NZ, NY, NX = 2, 4, 4


def place(z, y, x, c):
    return (z % NZ) * 32 + (y % NY) * 8 + (x % NX) * 2 + c


ALL = [(z, y, x, c) for z in range(NZ) for y in range(NY) for x in range(NX) for c in range(2)]


def along(c, first, second, z):
    return place(z, second, first, c) if c == 0 else place(z, first, second, c)


SWAP_CORE = [(place(z, y, x, c), place(z, y, x, 1 - c)) for z, y, x, c in ALL]
SWAP_Z = [(place(z, y, x, c), place(1 - z, y, x, c)) for z, y, x, c in ALL]
RING = [(c, z, p, q) for c in range(2) for z in range(2) for p in range(4) for q in range(4)]


def shift1(s):
    return [(along(c, p, q, z), along(c, (p + s) % 4, q, z)) for c, z, p, q in RING]


def shift2(s):
    return [(along(c, p, q, z), along(c, p, (q + s) % 4, z)) for c, z, p, q in RING]


def table():
    rows = np.zeros((64, 40), np.int32)
    for z, y, x, c in ALL:
        p, q = (x, y) if c == 0 else (y, x)
        row = [c]
        for s2 in range(4):
            for s1 in range(4):
                for j in range(2):
                    p1, q2 = (p - s1) % 4, (q - s2) % 4
                    yy, xx = (q2, p1) if c == 0 else (p1, q2)
                    row.append((z ^ j) * 16 + yy * 4 + xx)
        rows[place(z, y, x, c), : len(row)] = row
    return rows


TABLE = table()
KSTEPS = 4
BLOCKS = [(s2, s1, j) for j in (0, 1) for s2 in (0, 1, 3, 2) for s1 in (0, 1, 3, 2)]


def at(s2, s1, j):
    return 1 + (s2 * 4 + s1) * 2 + j


def encode_body(info, *refs):
    xs, (w_own, w_other, vec_own, vec_other, out, acc) = refs[:-6], refs[-6:]
    kb = xs[0].shape[1] // KSTEPS
    rows = [jnp.concatenate([x[:, k * kb : k * kb + kb] for x in xs], 0) for k in range(KSTEPS)]
    for i, (w, vec) in enumerate(((w_own, vec_own), (w_other, vec_other))):
        pre = vec[0:1, :]
        for k, x in enumerate(rows):
            pre = pre + jnp.dot(x, w[k * kb : k * kb + kb, :], preferred_element_type=jnp.float32)
        acc[0] = pre * jnp.clip((pre - vec[1:2, :]) / 0.25, 0.0, 1.0)
        for b, source in enumerate(BLOCKS):
            row = pl.multiple_of(info[at(*source)] * 8, 8)
            acc[1, pl.ds(row, 8), :] = acc[0, b * 8 : b * 8 + 8, :]
        col = pl.multiple_of((info[0] ^ i) * 256, 256)
        out[:, pl.ds(col, 256)] = acc[1].astype(jnp.bfloat16)


def encode(info, xs, w_own, w_other, vec_own, vec_other):
    args = [pltpu.with_memory_space_constraint(v, pltpu.VMEM) for v in (*xs, w_own, w_other, vec_own, vec_other)]
    vmem = pl.BlockSpec(memory_space=pltpu.VMEM)
    return pl.pallas_call(
        encode_body,
        out_shape=jax.ShapeDtypeStruct((256, 512), jnp.bfloat16),
        in_specs=[pl.BlockSpec(memory_space=pltpu.SMEM)] + [vmem] * len(args),
        out_specs=vmem,
        scratch_shapes=[pltpu.VMEM((2, 256, 256), jnp.float32)],
        compiler_params=pltpu.CompilerParams(vmem_limit_bytes=8 << 20),
        name="encode",
    )(info, *args)


def decode(info, pieces, offsets, w_own, w_other, acc, last=False):
    n_in = len(pieces) + 2 + (acc is not None)

    def body(info, *refs):
        acts, (wo, wp) = refs[: len(pieces)], refs[len(pieces) : len(pieces) + 2]
        out = refs[n_in]
        for h, w in ((0, wo), (1, wp)):
            total = None if acc is None else refs[n_in - 1][h]
            for a, off in zip(acts, offsets):
                for i in range(a.shape[0]):
                    col = pl.multiple_of(info[at(*off[i])] * 512, 512)
                    part = lax.dot_general(
                        w[:, pl.ds(col, 512)], a[i], (((1,), (1,)), ((), ())), preferred_element_type=jnp.float32
                    )
                    total = part if total is None else total + part
            out[h] = total
        if last:
            layer = info[39]
            for k, ref in enumerate(refs[n_in + 1 :]):
                for h in range(2):
                    row = pl.multiple_of(jnp.minimum(layer + k, 3) * 72, 8)
                    ref[h] = out[h, pl.ds(row, 72), :].astype(ref.dtype)

    vmem = pl.BlockSpec(memory_space=pltpu.VMEM)
    args = [*pieces, w_own, w_other] + ([] if acc is None else [acc])
    args = [pltpu.with_memory_space_constraint(v, pltpu.VMEM) for v in args]
    shapes = [jax.ShapeDtypeStruct((2, 288, 256), jnp.float32)]
    if last:
        shapes += [jax.ShapeDtypeStruct((2, 72, 256), jnp.bfloat16 if k else jnp.float32) for k in range(4)]
    return pl.pallas_call(
        body,
        out_shape=shapes,
        in_specs=[pl.BlockSpec(memory_space=pltpu.SMEM)] + [vmem] * len(args),
        out_specs=[vmem] * len(shapes),
        compiler_params=pltpu.CompilerParams(vmem_limit_bytes=8 << 20),
        name="decode",
    )(info, *args)


def total_body(own, one, two, three, bias, mine, theirs):
    for h, out in ((0, mine), (1, theirs)):
        total = own[h] + one[h].astype(jnp.float32) + two[h].astype(jnp.float32) + three[h].astype(jnp.float32)
        out[...] = (total + bias[h][:, 0:1]).astype(jnp.bfloat16)


def sum_up(own, earlier, bias):
    vmem = pl.BlockSpec(memory_space=pltpu.VMEM)
    return pl.pallas_call(
        total_body,
        out_shape=[jax.ShapeDtypeStruct(own.shape[1:], jnp.bfloat16)] * 2,
        in_specs=[vmem] * 5,
        out_specs=[vmem] * 2,
        compiler_params=pltpu.CompilerParams(vmem_limit_bytes=4 << 20),
        name="sum_up",
    )(own, *earlier, bias)


def finish_body(move, mine, theirs, out):
    moved = jnp.dot(mine[...], move[0], preferred_element_type=jnp.float32)
    out[...] = (moved + jnp.dot(theirs[...], move[1], preferred_element_type=jnp.float32)).astype(jnp.bfloat16)


def finish(move, mine, theirs):
    vmem = pl.BlockSpec(memory_space=pltpu.VMEM)
    return pl.pallas_call(
        finish_body,
        out_shape=jax.ShapeDtypeStruct((mine.shape[0], 512), jnp.bfloat16),
        in_specs=[vmem] * 3,
        out_specs=vmem,
        compiler_params=pltpu.CompilerParams(vmem_limit_bytes=4 << 20),
        name="finish",
    )(move, mine, theirs)


def fetch_body(info, src, src2, dst, dst2, move):
    pltpu.sync_copy(src, dst)
    pltpu.sync_copy(src2, dst2)
    held, token = (lax.broadcasted_iota(jnp.int32, (256, 512), d) for d in (0, 1))
    for i in range(2):
        here = token == (held // 8 * 2 + (info[0] ^ i)) * 8 + held % 8
        move[i] = jnp.where(here, 1.0, 0.0).astype(jnp.bfloat16)


def fetch(info, *xs):
    return pl.pallas_call(
        fetch_body,
        out_shape=[jax.ShapeDtypeStruct(x.shape, x.dtype) for x in xs]
        + [jax.ShapeDtypeStruct((2, 256, 512), jnp.bfloat16)],
        in_specs=[pl.BlockSpec(memory_space=pltpu.SMEM)] + [pl.BlockSpec(memory_space=pl.ANY)] * 2,
        out_specs=[pl.BlockSpec(memory_space=pltpu.VMEM)] * 3,
        compiler_params=pltpu.CompilerParams(vmem_limit_bytes=4 << 20),
        name="fetch",
    )(info, *xs)


def work(residuals, enc_weight, enc_bias, thresh_levels, dec_weight, dec_bias):
    me, my_layer = lax.axis_index("feat"), lax.axis_index("layer")
    info = lax.dynamic_index_in_dim(jnp.asarray(TABLE), me, 0, keepdims=False).at[39].set(my_layer)
    layers, width, features = dec_weight.shape[1:]

    def send(x, pairs):
        return lax.ppermute(x, "feat", pairs)

    def join(*xs):
        return jnp.concatenate(xs, 0)

    resid = residuals[0].astype(jnp.float32)
    factor = lax.rsqrt(jnp.mean(resid * resid, axis=-1, keepdims=True) + 1e-06)
    normed = (resid * factor).astype(jnp.bfloat16)
    nz = send(normed, SWAP_Z)
    m = join(*(send(normed, shift1(s)) for s in (1, 3, 2)))
    mz = send(m, SWAP_Z)
    p, q = join(normed, m), join(nz, mz)
    rows = [x for v in (p, q) for x in [v] + [send(v, shift2(s)) for s in (1, 3, 2)]]

    wide_bias = jnp.pad(dec_bias, ((0, 0), (0, 256 - width)))
    vec = jnp.pad(join(enc_bias, thresh_levels.astype(jnp.float32) * 0.125, wide_bias), ((0, 5), (0, 0)))
    vec_other = send(vec, SWAP_CORE)
    enc_own = enc_weight[0]
    dec_own = dec_weight[0].reshape(layers * width, features)
    dec_other, enc_other, move = fetch(info, send(dec_own, SWAP_CORE), send(enc_own, SWAP_CORE))

    acts = encode(info, rows, enc_own, enc_other, vec, vec_other)

    own = acts[None]
    a1, a3, z0, a2 = (
        send(own, to)
        for to in (shift1(1), shift1(3), SWAP_Z, shift1(2))
    )
    lo, ro = send(own, shift2(1)), send(own, shift2(3))
    z1, z3 = send(a1, SWAP_Z), send(a3, SWAP_Z)
    h = join(a1, a3)
    rh, lh = send(h, shift2(3)), send(h, shift2(1))
    g = join(a2, z0)
    lg, rg = send(g, shift2(1)), send(g, shift2(3))
    za2, zl, zr = (send(x, SWAP_Z) for x in (a2, lg[:1], rg[:1]))
    farh = send(rh, shift2(3))
    k = join(z1, z3)
    lk, rk = send(k, shift2(1)), send(k, shift2(3))
    faro, farg = send(lo, shift2(1)), send(rg, shift2(3))
    fark, farb = send(lk, shift2(1)), send(zl, shift2(1))

    o_at, h_at, g_at, k_at, b_at = ((0, 0),), ((1, 0), (3, 0)), ((2, 0), (0, 1)), ((1, 1), (3, 1)), ((2, 1),)
    plan = (
        ((own, 0, o_at), (h, 0, h_at), (g, 0, g_at), (k, 0, k_at), (za2, 0, b_at)),
        ((lo, 1, o_at), (ro, 3, o_at), (rh, 3, h_at), (lh, 1, h_at), (rg, 3, g_at)),
        ((lg, 1, g_at), (farh, 2, h_at), (faro, 2, o_at), (lk, 1, k_at), (zl, 1, b_at)),
        ((rk, 3, k_at), (zr, 3, b_at)),
        ((farg, 2, g_at),),
        ((fark, 2, k_at), (farb, 2, b_at)),
    )
    bias = jnp.stack([vec[2, :width], vec_other[2, :width]])
    bias = jnp.broadcast_to(bias[:, :, None], (2, width, 128))

    part = None
    for n, group in enumerate(plan):
        if n == 3:
            part, bias = lax.optimization_barrier((part, bias))
        part, *sent = decode(
            info,
            [x for x, _, _ in group],
            [[(s2, *w) for w in where] for _, s2, where in group],
            dec_own,
            dec_other,
            part,
            last=n == len(plan) - 1,
        )

    own_part, *later = sent
    earlier = []
    for k, x in enumerate(later, 1):
        earlier.append(lax.ppermute(x, "layer", [(n, n + k) for n in range(layers - k)]))
    mine, theirs = sum_up(own_part, earlier, bias)

    return finish(move, mine, send(theirs, SWAP_CORE)).T[None]


def solution(mesh):
    in_specs = (
        P("layer", "feat", None),
        P("layer", None, "feat"),
        P("layer", "feat"),
        P("layer", "feat"),
        P("layer", None, "feat", None),
        P("layer", "feat"),
    )
    out_specs = P("layer", None, "feat")
    return jax.shard_map(work, mesh=mesh, in_specs=in_specs, out_specs=out_specs, check_vma=False)
```

```python
import jax
import jax.numpy as jnp
import numpy as np
from jax import lax
from jax.experimental import pallas as pl
from jax.experimental.pallas import tpu as pltpu
from jax.sharding import PartitionSpec as P


NZ, NY, NX = 2, 4, 4


def place(z, y, x, c):
    return (z % NZ) * 32 + (y % NY) * 8 + (x % NX) * 2 + c


ALL = [(z, y, x, c) for z in range(NZ) for y in range(NY) for x in range(NX) for c in range(2)]


def along(c, first, second, z):
    return place(z, second, first, c) if c == 0 else place(z, first, second, c)


SWAP_CORE = [(place(z, y, x, c), place(z, y, x, 1 - c)) for z, y, x, c in ALL]
SWAP_Z = [(place(z, y, x, c), place(1 - z, y, x, c)) for z, y, x, c in ALL]
RING = [(c, z, p, q) for c in range(2) for z in range(2) for p in range(4) for q in range(4)]


def shift1(s):
    return [(along(c, p, q, z), along(c, (p + s) % 4, q, z)) for c, z, p, q in RING]


def shift2(s):
    return [(along(c, p, q, z), along(c, p, (q + s) % 4, z)) for c, z, p, q in RING]


def table():
    rows = np.zeros((64, 40), np.int32)
    for z, y, x, c in ALL:
        p, q = (x, y) if c == 0 else (y, x)
        row = [c]
        for s2 in range(4):
            for s1 in range(4):
                for j in range(2):
                    p1, q2 = (p - s1) % 4, (q - s2) % 4
                    yy, xx = (q2, p1) if c == 0 else (p1, q2)
                    row.append((z ^ j) * 16 + yy * 4 + xx)
        rows[place(z, y, x, c), : len(row)] = row
    return rows


TABLE = table()
KSTEPS = 4
BLOCKS = [(s2, s1, j) for j in (0, 1) for s2 in (0, 1, 3, 2) for s1 in (0, 1, 3, 2)]


def at(s2, s1, j):
    return 1 + (s2 * 4 + s1) * 2 + j


def encode_body(info, *refs):
    xs, (w_own, w_other, vec_own, vec_other, out, acc) = refs[:-6], refs[-6:]
    kb = xs[0].shape[1] // KSTEPS
    rows = [jnp.concatenate([x[:, k * kb : k * kb + kb] for x in xs], 0) for k in range(KSTEPS)]
    for i, (w, vec) in enumerate(((w_own, vec_own), (w_other, vec_other))):
        pre = vec[0:1, :]
        for k, x in enumerate(rows):
            pre = pre + jnp.dot(x, w[k * kb : k * kb + kb, :], preferred_element_type=jnp.float32)
        acc[0] = pre * jnp.clip((pre - vec[1:2, :]) / 0.25, 0.0, 1.0)
        for b, source in enumerate(BLOCKS):
            row = pl.multiple_of(info[at(*source)] * 8, 8)
            acc[1, pl.ds(row, 8), :] = acc[0, b * 8 : b * 8 + 8, :]
        col = pl.multiple_of((info[0] ^ i) * 256, 256)
        out[:, pl.ds(col, 256)] = acc[1].astype(jnp.bfloat16)


def encode(info, xs, w_own, w_other, vec_own, vec_other):
    args = [pltpu.with_memory_space_constraint(v, pltpu.VMEM) for v in (*xs, w_own, w_other, vec_own, vec_other)]
    vmem = pl.BlockSpec(memory_space=pltpu.VMEM)
    return pl.pallas_call(
        encode_body,
        out_shape=jax.ShapeDtypeStruct((256, 512), jnp.bfloat16),
        in_specs=[pl.BlockSpec(memory_space=pltpu.SMEM)] + [vmem] * len(args),
        out_specs=vmem,
        scratch_shapes=[pltpu.VMEM((2, 256, 256), jnp.float32)],
        compiler_params=pltpu.CompilerParams(vmem_limit_bytes=8 << 20),
        name="encode",
    )(info, *args)


def decode(info, pieces, offsets, w_own, w_other, acc, last=False):
    n_in = len(pieces) + 2 + (acc is not None)

    def body(info, *refs):
        acts, (wo, wp) = refs[: len(pieces)], refs[len(pieces) : len(pieces) + 2]
        out = refs[n_in]
        for h, w in ((0, wo), (1, wp)):
            total = None if acc is None else refs[n_in - 1][h]
            for a, off in zip(acts, offsets):
                for i in range(a.shape[0]):
                    col = pl.multiple_of(info[at(*off[i])] * 512, 512)
                    part = lax.dot_general(
                        w[:, pl.ds(col, 512)], a[i], (((1,), (1,)), ((), ())), preferred_element_type=jnp.float32
                    )
                    total = part if total is None else total + part
            out[h] = total
        if last:
            layer = info[39]
            for k, ref in enumerate(refs[n_in + 1 :]):
                for h in range(2):
                    row = pl.multiple_of(jnp.minimum(layer + k, 3) * 72, 8)
                    ref[h] = out[h, pl.ds(row, 72), :].astype(ref.dtype)

    vmem = pl.BlockSpec(memory_space=pltpu.VMEM)
    args = [*pieces, w_own, w_other] + ([] if acc is None else [acc])
    args = [pltpu.with_memory_space_constraint(v, pltpu.VMEM) for v in args]
    shapes = [jax.ShapeDtypeStruct((2, 288, 256), jnp.float32)]
    if last:
        shapes += [jax.ShapeDtypeStruct((2, 72, 256), jnp.bfloat16 if k else jnp.float32) for k in range(4)]
    return pl.pallas_call(
        body,
        out_shape=shapes,
        in_specs=[pl.BlockSpec(memory_space=pltpu.SMEM)] + [vmem] * len(args),
        out_specs=[vmem] * len(shapes),
        compiler_params=pltpu.CompilerParams(vmem_limit_bytes=8 << 20),
        name="decode",
    )(info, *args)


def total_body(own, one, two, three, bias, mine, theirs):
    for h, out in ((0, mine), (1, theirs)):
        total = own[h] + one[h].astype(jnp.float32) + two[h].astype(jnp.float32) + three[h].astype(jnp.float32)
        out[...] = (total + bias[h][:, 0:1]).astype(jnp.bfloat16)


def sum_up(own, earlier, bias):
    vmem = pl.BlockSpec(memory_space=pltpu.VMEM)
    return pl.pallas_call(
        total_body,
        out_shape=[jax.ShapeDtypeStruct(own.shape[1:], jnp.bfloat16)] * 2,
        in_specs=[vmem] * 5,
        out_specs=[vmem] * 2,
        compiler_params=pltpu.CompilerParams(vmem_limit_bytes=4 << 20),
        name="sum_up",
    )(own, *earlier, bias)


def finish_body(move, mine, theirs, out):
    moved = jnp.dot(mine[...], move[0], preferred_element_type=jnp.float32)
    out[...] = (moved + jnp.dot(theirs[...], move[1], preferred_element_type=jnp.float32)).astype(jnp.bfloat16)


def finish(move, mine, theirs):
    vmem = pl.BlockSpec(memory_space=pltpu.VMEM)
    return pl.pallas_call(
        finish_body,
        out_shape=jax.ShapeDtypeStruct((mine.shape[0], 512), jnp.bfloat16),
        in_specs=[vmem] * 3,
        out_specs=vmem,
        compiler_params=pltpu.CompilerParams(vmem_limit_bytes=4 << 20),
        name="finish",
    )(move, mine, theirs)


def fetch_body(info, src, src2, dst, dst2, move, sems):
    copies = [pltpu.make_async_copy(src, dst, sems.at[0]), pltpu.make_async_copy(src2, dst2, sems.at[1])]
    for copy in copies:
        copy.start()
    held, token = (lax.broadcasted_iota(jnp.int32, (256, 512), d) for d in (0, 1))
    for i in range(2):
        here = token == (held // 8 * 2 + (info[0] ^ i)) * 8 + held % 8
        move[i] = jnp.where(here, 1.0, 0.0).astype(jnp.bfloat16)
    for copy in copies:
        copy.wait()


def fetch(info, *xs):
    return pl.pallas_call(
        fetch_body,
        out_shape=[jax.ShapeDtypeStruct(x.shape, x.dtype) for x in xs]
        + [jax.ShapeDtypeStruct((2, 256, 512), jnp.bfloat16)],
        in_specs=[pl.BlockSpec(memory_space=pltpu.SMEM)] + [pl.BlockSpec(memory_space=pl.ANY)] * 2,
        out_specs=[pl.BlockSpec(memory_space=pltpu.VMEM)] * 3,
        scratch_shapes=[pltpu.SemaphoreType.DMA((2,))],
        compiler_params=pltpu.CompilerParams(vmem_limit_bytes=4 << 20),
        name="fetch",
    )(info, *xs)


def work(residuals, enc_weight, enc_bias, thresh_levels, dec_weight, dec_bias):
    me, my_layer = lax.axis_index("feat"), lax.axis_index("layer")
    info = lax.dynamic_index_in_dim(jnp.asarray(TABLE), me, 0, keepdims=False).at[39].set(my_layer)
    layers, width, features = dec_weight.shape[1:]

    def send(x, pairs):
        return lax.ppermute(x, "feat", pairs)

    def join(*xs):
        return jnp.concatenate(xs, 0)

    resid = residuals[0].astype(jnp.float32)
    factor = lax.rsqrt(jnp.mean(resid * resid, axis=-1, keepdims=True) + 1e-06)
    normed = (resid * factor).astype(jnp.bfloat16)
    nz = send(normed, SWAP_Z)
    m = join(*(send(normed, shift1(s)) for s in (1, 3, 2)))
    mz = send(m, SWAP_Z)
    p, q = join(normed, m), join(nz, mz)
    rows = [x for v in (p, q) for x in [v] + [send(v, shift2(s)) for s in (1, 3, 2)]]

    wide_bias = jnp.pad(dec_bias, ((0, 0), (0, 256 - width)))
    vec = jnp.pad(join(enc_bias, thresh_levels.astype(jnp.float32) * 0.125, wide_bias), ((0, 5), (0, 0)))
    vec_other = send(vec, SWAP_CORE)
    enc_own = enc_weight[0]
    dec_own = dec_weight[0].reshape(layers * width, features)
    dec_other, enc_other, move = fetch(info, send(dec_own, SWAP_CORE), send(enc_own, SWAP_CORE))

    acts = encode(info, rows, enc_own, enc_other, vec, vec_other)

    own = acts[None]
    a1, a3, z0, a2 = (
        send(own, to)
        for to in (shift1(1), shift1(3), SWAP_Z, shift1(2))
    )
    lo, ro = send(own, shift2(1)), send(own, shift2(3))
    z1, z3 = send(a1, SWAP_Z), send(a3, SWAP_Z)
    h = join(a1, a3)
    rh, lh = send(h, shift2(3)), send(h, shift2(1))
    g = join(a2, z0)
    lg, rg = send(g, shift2(1)), send(g, shift2(3))
    za2, zl, zr = (send(x, SWAP_Z) for x in (a2, lg[:1], rg[:1]))
    farh = send(rh, shift2(3))
    k = join(z1, z3)
    lk, rk = send(k, shift2(1)), send(k, shift2(3))
    faro, farg = send(lo, shift2(1)), send(rg, shift2(3))
    fark, farb = send(lk, shift2(1)), send(zl, shift2(1))

    o_at, h_at, g_at, k_at, b_at = ((0, 0),), ((1, 0), (3, 0)), ((2, 0), (0, 1)), ((1, 1), (3, 1)), ((2, 1),)
    plan = (
        ((own, 0, o_at), (h, 0, h_at), (g, 0, g_at), (k, 0, k_at), (za2, 0, b_at)),
        ((lo, 1, o_at), (ro, 3, o_at), (rh, 3, h_at), (lh, 1, h_at), (rg, 3, g_at)),
        ((lg, 1, g_at), (farh, 2, h_at), (faro, 2, o_at), (lk, 1, k_at), (zl, 1, b_at)),
        ((rk, 3, k_at), (zr, 3, b_at)),
        ((farg, 2, g_at),),
        ((fark, 2, k_at), (farb, 2, b_at)),
    )
    bias = jnp.stack([vec[2, :width], vec_other[2, :width]])
    bias = jnp.broadcast_to(bias[:, :, None], (2, width, 128))

    part = None
    for n, group in enumerate(plan):
        if n == 3:
            part, bias = lax.optimization_barrier((part, bias))
        part, *sent = decode(
            info,
            [x for x, _, _ in group],
            [[(s2, *w) for w in where] for _, s2, where in group],
            dec_own,
            dec_other,
            part,
            last=n == len(plan) - 1,
        )

    own_part, *later = sent
    earlier = []
    for k, x in enumerate(later, 1):
        earlier.append(lax.ppermute(x, "layer", [(n, n + k) for n in range(layers - k)]))
    mine, theirs = sum_up(own_part, earlier, bias)

    return finish(move, mine, send(theirs, SWAP_CORE)).T[None]


def solution(mesh):
    in_specs = (
        P("layer", "feat", None),
        P("layer", None, "feat"),
        P("layer", "feat"),
        P("layer", "feat"),
        P("layer", None, "feat", None),
        P("layer", "feat"),
    )
    out_specs = P("layer", None, "feat")
    return jax.shard_map(work, mesh=mesh, in_specs=in_specs, out_specs=out_specs, check_vma=False)
```
